512 devices in a mesh: occ: 64 (over y, x, core), vir: 8 (over z).
Axes of the slice: x: 4, y: 8, z: 8, core: 2. Of those that a mesh axis runs over, the one named last changes fastest.
Arguments:
- amplitudes: bfloat16 [32768, 64, 128], P(('occ', 'vir')), may hold values from -6 to 6
- tile_list: int32 [32768, 4], P(('occ', 'vir')), may hold values from 0 to 399, as said below
- ladder_virtual_integrals: bfloat16 [32, 64, 64], P('vir'), may hold values from -0.75 to 0.75
- ladder_domain_integrals: bfloat16 [16, 128, 128], P('vir'), may hold values from -0.5 to 0.5
- cycle_virtual: bfloat16 [16, 128, 128], P('vir'), may hold values from -0.5 to 0.5
- cycle_occupied: bfloat16 [400, 128], replicated, may hold values from -5 to 5
- cycle_core: bfloat16 [128, 128], replicated, may hold values from -0.5 to 0.5
- occ_energy: float32 [400], replicated, may hold values from -1.5 to -0.5
- vir_energy: float32 [2048], replicated, may hold values from 0.25 to 2
Outputs:
- updated: bfloat16 [32768, 64, 128], P(('occ', 'vir'))
The draws below stay inside these ranges and needn't reach their ends.
Inputs may be any that keep to these rules, and one draw needn't show every extreme that they name: `tile_list`: the tiles of device (o, v), rows (o * 8 + v) * 64 onward, have A from v * 4 to (v + 1) * 4 - 1 and g below 16; i and k lie below 400. Among one device's tiles at most 2 share the value of i modulo 64, and every device has such a value shared by exactly 2 of its tiles.
All inputs are finite; a program needn't handle non-finite values.
Results may differ from the reference program's by a relative error of at most 0.0057.
Values may be sent and summed in bfloat16 or wider, within the bound.
No kernel may reach another device: no remote copies, remote signals or barrier semaphores. Data moves between devices by JAX's collectives and lax.ppermute only.
A program may use at most 64 MiB of HBM per device.

```python
import jax
import jax.numpy as jnp
from jax import lax

O = 400
V = 2048
TW = 64
DOM = 128
R = 128
TILE_DEV = 64
NTILE = 32768
NVT = 32
NVL = 4
NDOM = 16
OWNERS = 64
CAP = 2


def draw_tile_list(key, part):
    blocks = NTILE // TILE_DEV
    vir_count = NVT // NVL
    subkeys = jax.random.split(key, 8)
    block_ids = jnp.arange(blocks, dtype=jnp.int32)
    vir_of = block_ids % vir_count
    favored = jax.random.randint(subkeys[0], (vir_count,), 0, OWNERS, dtype=jnp.int32)[vir_of]
    owner_perm = jax.vmap(lambda sub_key: jax.random.permutation(sub_key, OWNERS))(jax.random.split(subkeys[1], blocks)).astype(jnp.int32)
    where_fav = jnp.argmax(owner_perm == favored[:, None], axis=1)
    leading = owner_perm[:, 0]
    block_rows = jnp.arange(blocks)
    owner_perm = owner_perm.at[block_rows, where_fav].set(leading)
    owner_perm = owner_perm.at[block_rows, 0].set(favored)
    spare_count = jax.random.randint(subkeys[2], (blocks, OWNERS), 1, CAP + 1, dtype=jnp.int32)
    even_slot = jnp.arange(OWNERS, dtype=jnp.int32) % 2 == 0
    counts = jnp.where(even_slot[None, :], CAP, spare_count).astype(jnp.int32)
    bounds = jnp.cumsum(counts, axis=1)
    positions = jnp.arange(TILE_DEV, dtype=jnp.int32)
    owner_pos = jnp.sum((bounds[:, None, :] <= positions[None, :, None]).astype(jnp.int32), axis=2)
    target = jnp.take_along_axis(owner_perm, owner_pos, axis=1)
    multiple = jax.random.randint(subkeys[3], (blocks, TILE_DEV), 0, O // OWNERS, dtype=jnp.int32)
    first_occ = target + OWNERS * multiple
    second_occ = jax.random.randint(subkeys[4], (blocks, TILE_DEV), 0, O, dtype=jnp.int32)
    second_occ = jnp.where(positions[None, :] == 0, O - 1, second_occ)
    second_occ = jnp.where(positions[None, :] == 1, 0, second_occ)
    virtual_tile = vir_of[:, None] * NVL + jax.random.randint(subkeys[5], (blocks, TILE_DEV), 0, NVL, dtype=jnp.int32)
    pair_domain = jax.random.randint(subkeys[6], (blocks, TILE_DEV), 0, NDOM, dtype=jnp.int32)
    shuffle = jax.vmap(lambda sub_key: jax.random.permutation(sub_key, TILE_DEV))(jax.random.split(subkeys[7], blocks)).astype(jnp.int32)
    stacked = jnp.stack([first_occ, second_occ, virtual_tile, pair_domain], axis=2).astype(jnp.int32)
    shuffled = jnp.take_along_axis(stacked, shuffle[:, :, None], axis=1)
    return shuffled.reshape(blocks * TILE_DEV, 4).astype(jnp.int32)


def block_scale(rng, extent, cuts, low, top_value):
    def one(position, shards_of):
        draws = jax.random.uniform(jax.random.fold_in(jax.random.fold_in(rng, 6), position), (shards_of,), jnp.float32, low / len(cuts), top_value / len(cuts))
        return jnp.repeat(jnp.exp(draws), extent[position] // shards_of).reshape((-1,) + (1,) * (len(extent) - position - 1))

    factor_of = one(*cuts[0])
    for cut in cuts[1:]:
        factor_of = factor_of * one(*cut)
    return factor_of


def normal_values(stream_key, dims, scale, bound, cuts=(), kind=jnp.bfloat16):
    drawn = jax.random.normal(stream_key, dims, jnp.float32) * scale
    if len(cuts) > 0:
        drawn = block_scale(stream_key, dims, cuts, -0.22, 0.18) * drawn
    return jnp.clip(drawn, min=-bound, max=bound).astype(kind)


def setup_inputs(seed: int = 0) -> dict:
    keys = jax.random.split(jax.random.key(seed), 10)
    amplitudes = normal_values(keys[0], (NTILE, TW, DOM), 1.0, 6.0, ((0, 512),))
    tile_list = draw_tile_list(jax.random.fold_in(keys[9], 71), 0)
    ladder_virtual_integrals = normal_values(keys[2], (NVT, TW, TW), TW ** -0.5, 0.75, ((0, 8),))
    ladder_domain_integrals = normal_values(keys[3], (NDOM, DOM, DOM), DOM ** -0.5, 0.5, ((0, 8),))
    cycle_virtual = normal_values(keys[4], (NDOM, DOM, R), DOM ** -0.5, 0.5, ((0, 8),))
    cycle_occupied = normal_values(keys[5], (O, R), 1.0, 5.0)
    cycle_core = normal_values(keys[6], (R, R), R ** -0.5, 0.5)
    occ_energy = jnp.clip(jax.random.uniform(keys[7], (O,), jnp.float32, -1.5, -0.5), -1.5, -0.5)
    vir_energy = jnp.clip(jax.random.uniform(keys[8], (V,), jnp.float32, 0.25, 2.0), 0.25, 2.0)
    return dict(amplitudes=amplitudes, tile_list=tile_list, ladder_virtual_integrals=ladder_virtual_integrals, ladder_domain_integrals=ladder_domain_integrals, cycle_virtual=cycle_virtual, cycle_occupied=cycle_occupied, cycle_core=cycle_core, occ_energy=occ_energy, vir_energy=vir_energy)


def make_factors(cycle_virtual, cycle_occupied, second_occ, pair_domain):
    scaled = cycle_virtual[pair_domain].astype(jnp.float32) * cycle_occupied[second_occ].astype(jnp.float32)[:, None, :]
    return scaled.astype(jnp.bfloat16)


def reference(amplitudes, tile_list, ladder_virtual_integrals, ladder_domain_integrals, cycle_virtual, cycle_occupied, cycle_core, occ_energy, vir_energy):
    tile_total = amplitudes.shape[0]
    vir_tiles = V // TW
    blocks = tile_total // TILE_DEV
    amp_blocks = amplitudes.reshape(blocks, TILE_DEV, TW, DOM)
    list_blocks = tile_list.reshape(blocks, TILE_DEV, 4)

    def project(pieces):
        amplitude_portion, list_part = pieces
        cycle_factors = make_factors(cycle_virtual, cycle_occupied, list_part[:, 1], list_part[:, 3])
        return jnp.einsum("xge,xew->xgw", amplitude_portion.astype(jnp.float32), cycle_factors.astype(jnp.float32)).astype(jnp.bfloat16)

    partial_value = lax.map(project, (amp_blocks, list_blocks)).reshape(tile_total, TW, R)
    group_key = (tile_list[:, 0] * vir_tiles + tile_list[:, 2]).astype(jnp.int32)
    group_sums = jax.ops.segment_sum(partial_value.astype(jnp.float32), group_key, num_segments=O * vir_tiles)
    group_sums = group_sums.astype(jnp.bfloat16)
    group_core = jnp.dot(group_sums.reshape(-1, R).astype(jnp.float32), cycle_core.astype(jnp.float32))
    group_core = group_core.astype(jnp.bfloat16).reshape(O * vir_tiles, TW, R)

    def update(pieces):
        amplitude_portion, list_part = pieces
        first_occ = list_part[:, 0]
        second_occ = list_part[:, 1]
        virtual_tile = list_part[:, 2]
        pair_domain = list_part[:, 3]
        cycle_factors = make_factors(cycle_virtual, cycle_occupied, second_occ, pair_domain)
        midpoint_result = jnp.einsum("fnd,fdg->fng", amplitude_portion.astype(jnp.float32), ladder_domain_integrals[pair_domain].astype(jnp.float32)).astype(jnp.bfloat16)
        ladder_contribution = jnp.einsum("fnd,fdg->fng", ladder_virtual_integrals[virtual_tile].astype(jnp.float32), midpoint_result.astype(jnp.float32))
        own_core = group_core[first_occ * vir_tiles + virtual_tile]
        cycle_term = jnp.einsum("tar,tbr->tab", own_core.astype(jnp.float32), cycle_factors.astype(jnp.float32)).astype(jnp.bfloat16)
        rows_left = virtual_tile[:, None] * TW + jnp.arange(TW, dtype=jnp.int32)[None, :]
        rows_right = pair_domain[:, None] * DOM + jnp.arange(DOM, dtype=jnp.int32)[None, :]
        occ_sum = occ_energy[first_occ] + occ_energy[second_occ]
        denominator = vir_energy[rows_left][:, :, None] + vir_energy[rows_right][:, None, :] - occ_sum[:, None, None]
        result = amplitude_portion.astype(jnp.float32) + (ladder_contribution + cycle_term.astype(jnp.float32)) / denominator
        return result.astype(jnp.bfloat16)

    updated = lax.map(update, (amp_blocks, list_blocks))
    return updated.reshape(tile_total, TW, DOM)
```

```python
import jax
import jax.numpy as jnp
from jax import lax
from jax.experimental import pallas as pl
from jax.experimental.pallas import tpu as pltpu
from jax.sharding import PartitionSpec as P

CAP = 2
META = 8
SMEM = pltpu.SMEM
VMEM = pltpu.VMEM


def sds(shape, dtype):
    return jax.ShapeDtypeStruct(shape, dtype)


def spec(space=VMEM):
    return pl.BlockSpec(memory_space=space)


def pack(amplitudes, tile_list, owners, local_tiles, empty_key):
    tiles, width, domain = amplitudes.shape
    rows = CAP * width

    def kernel(list_ref, amp_ref, out_ref, pos_ref, count, meta):
        out_ref[...] = jnp.zeros_like(out_ref)
        lane = lax.broadcasted_iota(jnp.int32, (1, domain), 1)
        empty = jnp.where(lax.broadcasted_iota(jnp.int32, meta.shape, 1) % 4 == 0, empty_key, 0)
        meta[...] = empty.astype(jnp.float32)

        def clear(o, carry):
            count[o] = 0
            return carry

        lax.fori_loop(0, owners, clear, 0, unroll=8)

        def place(t, carry):
            i = list_ref[t, 0]
            k = list_ref[t, 1]
            owner = lax.rem(i, owners)
            rank = count[owner]
            count[owner] = rank + 1
            pos_ref[t] = owner * CAP + rank
            key = lax.div(i, owners) * local_tiles + lax.rem(list_ref[t, 2], local_tiles)
            row = meta[pl.ds(owner * META, 1), :]
            field = lane - 4 * rank
            row = jnp.where(field == 0, key.astype(jnp.float32), row)
            row = jnp.where(field == 1, lax.div(k, 16).astype(jnp.float32), row)
            row = jnp.where(field == 2, lax.rem(k, 16).astype(jnp.float32), row)
            row = jnp.where(field == 3, list_ref[t, 3].astype(jnp.float32), row)
            meta[pl.ds(owner * META, 1), :] = row
            out_ref[owner, pl.ds(pl.multiple_of(rank * width, width), width), :] = amp_ref[t]
            return carry

        lax.fori_loop(0, tiles, place, 0, unroll=4)
        out_ref[:, rows:, :] = meta[...].reshape(owners, META, domain).astype(jnp.bfloat16)

    return pl.pallas_call(
        kernel,
        out_shape=(sds((owners, rows + META, domain), jnp.bfloat16), sds((tiles,), jnp.int32)),
        in_specs=[spec(SMEM), spec()],
        out_specs=(spec(), spec(SMEM)),
        scratch_shapes=[SMEM((owners,), jnp.int32), VMEM((owners * META, domain), jnp.float32)],
        name="pack",
    )(tile_list, amplitudes)


def owner_core(received, cycle_virtual, cycle_occupied, cycle_core, width, groups):
    sources, message, domain = received.shape
    rank = cycle_core.shape[0]
    rows = CAP * width

    def kernel(got_ref, cv_ref, co_ref, core_ref, out_ref, meta, ids_v, ids, sums, cores, sem):
        got_meta = got_ref[:, rows:, :].astype(jnp.float32)
        meta[...] = got_meta.reshape(meta.shape)
        ids_v[...] = meta[pl.ds(0, sources, stride=META), :].astype(jnp.int32)
        copy = pltpu.make_async_copy(ids_v, ids, sem)
        copy.start()
        sums[...] = jnp.zeros_like(sums)
        copy.wait()

        def add(s, carry):
            for c in range(CAP):
                key = ids[s, 4 * c]
                k = ids[s, 4 * c + 1] * 16 + ids[s, 4 * c + 2]
                g = ids[s, 4 * c + 3]
                tile = got_ref[s, c * width : (c + 1) * width, :]
                part = jnp.dot(tile, cv_ref[g], preferred_element_type=jnp.float32)
                part = part * co_ref[pl.ds(k, 1), :]
                sums[key] += part.astype(jnp.bfloat16).astype(jnp.float32)
            return carry

        lax.fori_loop(0, sources, add, 0, unroll=4)
        grouped = sums[...].astype(jnp.bfloat16).reshape((groups + 1) * width, rank)
        core = jnp.dot(grouped, core_ref[...], preferred_element_type=jnp.float32)
        cores[...] = core.astype(jnp.bfloat16).reshape(cores.shape)

        def answer(s, carry):
            for c in range(CAP):
                out_ref[s, c * width : (c + 1) * width, :] = cores[ids[s, 4 * c]]
            return carry

        lax.fori_loop(0, sources, answer, 0, unroll=4)

    return pl.pallas_call(
        kernel,
        out_shape=sds((sources, rows, rank), jnp.bfloat16),
        in_specs=[spec()] * 4,
        out_specs=spec(),
        scratch_shapes=[
            VMEM((sources * META, domain), jnp.float32),
            VMEM((sources, domain), jnp.int32),
            SMEM((sources, domain), jnp.int32),
            VMEM((groups + 1, width, rank), jnp.float32),
            VMEM((groups + 1, width, rank), jnp.bfloat16),
            pltpu.SemaphoreType.DMA,
        ],
        name="owner_core",
    )(received, cycle_virtual, cycle_occupied.astype(jnp.float32), cycle_core)


def ladder_part(tile_list, occ_energy, amplitudes, ladder_virtual, ladder_domain, row_energy, column_energy):
    tiles, width, domain = amplitudes.shape
    local_tiles = ladder_virtual.shape[0]

    def kernel(list_ref, occ_ref, amp_ref, lv_ref, ld_ref, re_ref, ce_ref, base_ref, inv_ref):
        def one(t, carry):
            a = lax.rem(list_ref[t, 2], local_tiles)
            g = list_ref[t, 3]
            amp = amp_ref[t]
            half = jnp.dot(amp, ld_ref[g], preferred_element_type=jnp.float32).astype(jnp.bfloat16)
            ladder = jnp.dot(lv_ref[a], half, preferred_element_type=jnp.float32)
            occ = occ_ref[list_ref[t, 0]] + occ_ref[list_ref[t, 1]]
            inverse = 1.0 / (re_ref[a] + ce_ref[pl.ds(g, 1), :] - occ)
            base_ref[t] = amp.astype(jnp.float32) + ladder * inverse
            inv_ref[t] = inverse
            return carry

        lax.fori_loop(0, tiles, one, 0, unroll=4)

    return pl.pallas_call(
        kernel,
        out_shape=(sds(amplitudes.shape, jnp.float32), sds(amplitudes.shape, jnp.float32)),
        in_specs=[spec(SMEM), spec(SMEM)] + [spec()] * 5,
        out_specs=(spec(), spec()),
        name="ladder",
    )(tile_list, occ_energy, amplitudes, ladder_virtual, ladder_domain, row_energy, column_energy)


def finish(tile_list, position, returned, cycle_virtual, cycle_occupied, base, inverse):
    tiles, width, domain = base.shape

    def kernel(list_ref, pos_ref, ret_ref, cv_ref, co_ref, base_ref, inv_ref, out_ref):
        def one(t, carry):
            slot = pos_ref[t]
            core = ret_ref[slot].astype(jnp.float32) * co_ref[pl.ds(list_ref[t, 1], 1), :]
            term = lax.dot_general(
                core.astype(jnp.bfloat16),
                cv_ref[list_ref[t, 3]],
                (((1,), (1,)), ((), ())),
                preferred_element_type=jnp.float32,
            )
            out_ref[t] = (base_ref[t] + term * inv_ref[t]).astype(jnp.bfloat16)
            return carry

        lax.fori_loop(0, tiles, one, 0, unroll=4)

    return pl.pallas_call(
        kernel,
        out_shape=sds(base.shape, jnp.bfloat16),
        in_specs=[spec(SMEM), spec(SMEM)] + [spec()] * 5,
        out_specs=spec(),
        name="finish",
    )(tile_list, position, returned, cycle_virtual, cycle_occupied.astype(jnp.float32), base, inverse)


def body(
    amplitudes,
    tile_list,
    ladder_virtual_integrals,
    ladder_domain_integrals,
    cycle_virtual,
    cycle_occupied,
    cycle_core,
    occ_energy,
    vir_energy,
):
    tiles, width, domain = amplitudes.shape
    owners = lax.axis_size("occ")
    local_tiles = ladder_virtual_integrals.shape[0]
    groups = -(-occ_energy.shape[0] // owners) * local_tiles
    vir_index = lax.axis_index("vir")
    local_energy = lax.dynamic_slice_in_dim(vir_energy, vir_index * local_tiles * width, local_tiles * width)
    row_energy = jnp.broadcast_to(local_energy.reshape(local_tiles, width, 1), (local_tiles, width, domain))
    column_energy = vir_energy.reshape(-1, domain)

    send, position = pack(amplitudes, tile_list, owners, local_tiles, groups)
    received = lax.all_to_all(send, "occ", split_axis=0, concat_axis=0, tiled=True)
    virtual_all = lax.all_gather(cycle_virtual, "vir", axis=0, tiled=True)
    answers = owner_core(received, virtual_all, cycle_occupied, cycle_core, width, groups)
    returned = lax.all_to_all(answers, "occ", split_axis=0, concat_axis=0, tiled=True)
    domain_own, _ = lax.optimization_barrier((ladder_domain_integrals, virtual_all))
    domain_all = lax.all_gather(domain_own, "vir", axis=0, tiled=True)
    base, inverse = ladder_part(
        tile_list, occ_energy, amplitudes, ladder_virtual_integrals, domain_all, row_energy, column_energy
    )
    return finish(
        tile_list,
        position,
        returned.reshape(owners * CAP, width, domain),
        virtual_all,
        cycle_occupied,
        base,
        inverse,
    )


def solution(mesh):
    tile_spec = P(("occ", "vir"), None, None)
    return jax.shard_map(
        body,
        mesh=mesh,
        in_specs=(tile_spec, P(("occ", "vir"), None), P("vir"), P("vir"), P("vir"), P(), P(), P(), P()),
        out_specs=tile_spec,
        check_vma=False,
    )
```

```python
import jax
import jax.numpy as jnp
from jax import lax
from jax.experimental import pallas as pl
from jax.experimental.pallas import tpu as pltpu
from jax.sharding import PartitionSpec as P

CAP = 2
META = 8
CHUNKS = 4
SMEM = pltpu.SMEM
VMEM = pltpu.VMEM


def sds(shape, dtype):
    return jax.ShapeDtypeStruct(shape, dtype)


def spec(space=VMEM):
    return pl.BlockSpec(memory_space=space)


def pack(amplitudes, tile_list, owners, local_tiles):
    tiles, width, domain = amplitudes.shape
    rows = CAP * width

    def kernel(list_ref, ids_ref, amp_ref, out_ref, pos_ref, count, meta, tile_sem, meta_sem):
        def clear(o, carry):
            count[o] = 0
            return carry

        lax.fori_loop(0, owners, clear, 0, unroll=8)

        def place(t, carry):
            owner = lax.rem(list_ref[0, t], owners)
            rank = count[owner]
            count[owner] = rank + 1
            pos_ref[t] = owner * CAP + rank
            slot = out_ref.at[owner, pl.ds(pl.multiple_of(rank * width, width), width)]
            pltpu.make_async_copy(amp_ref.at[t], slot, tile_sem).start()
            return carry

        lax.fori_loop(0, tiles, place, 0, unroll=4)
        ids = ids_ref[...]
        i, k = ids[0:1], ids[1:2]
        owner = jnp.broadcast_to(lax.rem(i, owners).astype(jnp.float32), (tiles, tiles))
        earlier = lax.broadcasted_iota(jnp.int32, (tiles, tiles), 0) < lax.broadcasted_iota(
            jnp.int32, (tiles, tiles), 1
        )
        same = jnp.where((owner == owner.T) & earlier, 1.0, 0.0)
        rank = jnp.sum(same, axis=0, keepdims=True)
        key = lax.div(i, owners) * local_tiles + lax.rem(ids[2:3], local_tiles) + 1
        fields = [v.astype(jnp.float32) for v in (key, lax.div(k, 16), lax.rem(k, 16), ids[3:4])]
        lane = lax.broadcasted_iota(jnp.int32, (domain, tiles), 0)
        row_owner = lax.broadcasted_iota(jnp.int32, (owners * META, tiles), 0) // META
        total = jnp.zeros((owners * META, domain), jnp.float32)
        for c in range(CAP):
            mine = (row_owner.astype(jnp.float32) == owner[0:1]) & (rank == float(c))
            table = jnp.zeros((domain, tiles), jnp.float32)
            for f, value in enumerate(fields):
                table = jnp.where(lane == 4 * c + f, value, table)
            total += lax.dot_general(
                jnp.where(mine, 1.0, 0.0).astype(jnp.bfloat16),
                table.astype(jnp.bfloat16),
                (((1,), (1,)), ((), ())),
                preferred_element_type=jnp.float32,
            )
        meta[...] = total.reshape(owners, META, domain).astype(jnp.bfloat16)
        meta_copy = pltpu.make_async_copy(meta, out_ref.at[:, pl.ds(rows, META)], meta_sem)
        meta_copy.start()
        meta_copy.wait()
        pltpu.make_async_copy(amp_ref, amp_ref, tile_sem).wait()

    return pl.pallas_call(
        kernel,
        out_shape=(sds((owners, rows + META, domain), jnp.bfloat16), sds((tiles,), jnp.int32)),
        in_specs=[spec(SMEM), spec(), spec(pl.ANY)],
        out_specs=(spec(pl.ANY), spec(SMEM)),
        scratch_shapes=[
            SMEM((owners,), jnp.int32),
            VMEM((owners, META, domain), jnp.bfloat16),
            pltpu.SemaphoreType.DMA,
            pltpu.SemaphoreType.DMA,
        ],
        name="pack",
    )(tile_list, tile_list, amplitudes)


def owner_core(received, cycle_virtual, cycle_occupied, cycle_core, width, groups):
    sources, message, domain = received.shape
    rank = cycle_core.shape[0]
    rows = CAP * width
    part = sources // CHUNKS

    def kernel(
        got_ref, cv_ref, co_ref, core_ref, out_ref, got, meta_b, meta, ids_v, ids, sums, cores, sem, meta_sem, out_sem
    ):
        meta_copy = pltpu.make_async_copy(got_ref.at[:, pl.ds(rows, META)], meta_b, meta_sem)
        meta_copy.start()
        copies = [
            pltpu.make_async_copy(
                got_ref.at[pl.ds(j * part, part), pl.ds(0, rows)], got.at[pl.ds(j * part, part)], sem.at[j]
            )
            for j in range(CHUNKS)
        ]
        for copy in copies:
            copy.start()
        sums[...] = jnp.zeros_like(sums)
        meta_copy.wait()
        meta[...] = meta_b[...].astype(jnp.float32).reshape(meta.shape)
        ids_v[...] = meta[pl.ds(0, sources, stride=META), :].astype(jnp.int32)
        ids_copy = pltpu.make_async_copy(ids_v, ids, meta_sem)
        ids_copy.start()
        ids_copy.wait()

        def add(s, carry):
            for c in range(CAP):
                key = ids[s, 4 * c]
                k = ids[s, 4 * c + 1] * 16 + ids[s, 4 * c + 2]
                g = ids[s, 4 * c + 3]
                tile = got[s, c * width : (c + 1) * width, :]
                one = jnp.dot(tile, cv_ref[g], preferred_element_type=jnp.float32)
                one = one * co_ref[pl.ds(k, 1), :]
                sums[key] += one.astype(jnp.bfloat16).astype(jnp.float32)
            return carry

        for j, copy in enumerate(copies):
            copy.wait()
            lax.fori_loop(j * part, (j + 1) * part, add, 0, unroll=4)
        grouped = sums[...].astype(jnp.bfloat16).reshape((groups + 1) * width, rank)
        core = jnp.dot(grouped, core_ref[...], preferred_element_type=jnp.float32)
        cores[...] = core.astype(jnp.bfloat16).reshape(cores.shape)

        def answer(s, carry):
            for c in range(CAP):
                slot = out_ref.at[s, pl.ds(c * width, width)]
                pltpu.make_async_copy(cores.at[ids[s, 4 * c]], slot, out_sem).start()
            return carry

        lax.fori_loop(0, sources, answer, 0, unroll=4)
        pltpu.make_async_copy(out_ref, out_ref, out_sem).wait()

    return pl.pallas_call(
        kernel,
        out_shape=sds((sources, rows, rank), jnp.bfloat16),
        in_specs=[spec(pl.ANY)] + [spec()] * 3,
        out_specs=spec(pl.ANY),
        scratch_shapes=[
            VMEM((sources, rows, domain), jnp.bfloat16),
            VMEM((sources, META, domain), jnp.bfloat16),
            VMEM((sources * META, domain), jnp.float32),
            VMEM((sources, domain), jnp.int32),
            SMEM((sources, domain), jnp.int32),
            VMEM((groups + 1, width, rank), jnp.float32),
            VMEM((groups + 1, width, rank), jnp.bfloat16),
            pltpu.SemaphoreType.DMA((CHUNKS,)),
            pltpu.SemaphoreType.DMA,
            pltpu.SemaphoreType.DMA,
        ],
        name="owner_core",
    )(received, cycle_virtual, cycle_occupied.astype(jnp.float32), cycle_core)


def ladder_part(tile_list, occ_energy, amplitudes, ladder_virtual, ladder_domain, row_energy, column_energy):
    tiles, width, domain = amplitudes.shape
    local_tiles = ladder_virtual.shape[0]

    def kernel(list_ref, occ_ref, amp_ref, lv_ref, ld_ref, re_ref, ce_ref, base_ref, inv_ref):
        def one(t, carry):
            a = lax.rem(list_ref[2, t], local_tiles)
            g = list_ref[3, t]
            amp = amp_ref[t]
            half = jnp.dot(amp, ld_ref[g], preferred_element_type=jnp.float32).astype(jnp.bfloat16)
            ladder = jnp.dot(lv_ref[a], half, preferred_element_type=jnp.float32)
            occ = occ_ref[list_ref[0, t]] + occ_ref[list_ref[1, t]]
            inverse = 1.0 / (re_ref[a] + ce_ref[pl.ds(g, 1), :] - occ)
            base_ref[t] = amp.astype(jnp.float32) + ladder * inverse
            inv_ref[t] = inverse
            return carry

        lax.fori_loop(0, tiles, one, 0, unroll=4)

    return pl.pallas_call(
        kernel,
        out_shape=(sds(amplitudes.shape, jnp.float32), sds(amplitudes.shape, jnp.float32)),
        in_specs=[spec(SMEM), spec(SMEM)] + [spec()] * 5,
        out_specs=(spec(), spec()),
        name="ladder",
    )(tile_list, occ_energy, amplitudes, ladder_virtual, ladder_domain, row_energy, column_energy)


def finish(tile_list, position, returned, cycle_virtual, cycle_occupied, base, inverse):
    tiles, width, domain = base.shape
    part = tiles // CHUNKS

    def kernel(
        list_ref, pos_ref, ret_ref, cv_ref, co_ref, base_ref, inv_ref, out_ref, core, base, inv, out, core_sem, sem, out_sem
    ):
        loads, stores = [], []
        for j in range(CHUNKS):
            piece = pl.ds(j * part, part)
            loads.append(
                (
                    pltpu.make_async_copy(base_ref.at[piece], base.at[piece], sem.at[j, 0]),
                    pltpu.make_async_copy(inv_ref.at[piece], inv.at[piece], sem.at[j, 1]),
                    pltpu.make_async_copy(ret_ref.at[piece], core.at[piece], core_sem.at[j]),
                )
            )
            stores.append(pltpu.make_async_copy(out.at[piece], out_ref.at[piece], out_sem.at[j]))

        for j in range(CHUNKS):

            def fetch(t, carry):
                pltpu.make_async_copy(ret_ref.at[pos_ref[t]], core.at[t], core_sem.at[j]).start()
                return carry

            lax.fori_loop(j * part, (j + 1) * part, fetch, 0, unroll=4)
            loads[j][0].start()
            loads[j][1].start()

        def one(t, carry):
            scaled = core[t].astype(jnp.float32) * co_ref[pl.ds(list_ref[1, t], 1), :]
            term = lax.dot_general(
                scaled.astype(jnp.bfloat16),
                cv_ref[list_ref[3, t]],
                (((1,), (1,)), ((), ())),
                preferred_element_type=jnp.float32,
            )
            out[t] = (base[t] + term * inv[t]).astype(jnp.bfloat16)
            return carry

        for j in range(CHUNKS):
            for copy in loads[j]:
                copy.wait()
            lax.fori_loop(j * part, (j + 1) * part, one, 0, unroll=4)
            stores[j].start()
        for copy in stores:
            copy.wait()

    return pl.pallas_call(
        kernel,
        out_shape=sds(base.shape, jnp.bfloat16),
        in_specs=[spec(SMEM), spec(SMEM), spec(pl.ANY), spec(), spec(), spec(pl.ANY), spec(pl.ANY)],
        out_specs=spec(pl.ANY),
        scratch_shapes=[
            VMEM((tiles, width, domain), jnp.bfloat16),
            VMEM((tiles, width, domain), jnp.float32),
            VMEM((tiles, width, domain), jnp.float32),
            VMEM((tiles, width, domain), jnp.bfloat16),
            pltpu.SemaphoreType.DMA((CHUNKS,)),
            pltpu.SemaphoreType.DMA((CHUNKS, 2)),
            pltpu.SemaphoreType.DMA((CHUNKS,)),
        ],
        name="finish",
    )(tile_list, position, returned, cycle_virtual, cycle_occupied.astype(jnp.float32), base, inverse)


def body(
    amplitudes,
    tile_list,
    ladder_virtual_integrals,
    ladder_domain_integrals,
    cycle_virtual,
    cycle_occupied,
    cycle_core,
    occ_energy,
    vir_energy,
):
    tiles, width, domain = amplitudes.shape
    owners = lax.axis_size("occ")
    local_tiles = ladder_virtual_integrals.shape[0]
    groups = -(-occ_energy.shape[0] // owners) * local_tiles
    vir_index = lax.axis_index("vir")
    local_energy = lax.dynamic_slice_in_dim(vir_energy, vir_index * local_tiles * width, local_tiles * width)
    row_energy = jnp.broadcast_to(local_energy.reshape(local_tiles, width, 1), (local_tiles, width, domain))
    column_energy = vir_energy.reshape(-1, domain)

    tile_list = tile_list.T
    send, position = pack(amplitudes, tile_list, owners, local_tiles)
    received = lax.all_to_all(send, "occ", split_axis=0, concat_axis=0, tiled=True)
    virtual_all = lax.all_gather(cycle_virtual, "vir", axis=0, tiled=True)
    answers = owner_core(received, virtual_all, cycle_occupied, cycle_core, width, groups)
    returned = lax.all_to_all(answers, "occ", split_axis=0, concat_axis=0, tiled=True)
    domain_own, _ = lax.optimization_barrier((ladder_domain_integrals, virtual_all))
    domain_all = lax.all_gather(domain_own, "vir", axis=0, tiled=True)
    base, inverse = ladder_part(
        tile_list, occ_energy, amplitudes, ladder_virtual_integrals, domain_all, row_energy, column_energy
    )
    return finish(
        tile_list,
        position,
        returned.reshape(owners * CAP, width, domain),
        virtual_all,
        cycle_occupied,
        base,
        inverse,
    )


def solution(mesh):
    tile_spec = P(("occ", "vir"), None, None)
    return jax.shard_map(
        body,
        mesh=mesh,
        in_specs=(tile_spec, P(("occ", "vir"), None), P("vir"), P("vir"), P("vir"), P(), P(), P(), P()),
        out_specs=tile_spec,
        check_vma=False,
    )
```

```python
import jax
import jax.numpy as jnp
from jax import lax
from jax.experimental import pallas as pl
from jax.experimental.pallas import tpu as pltpu
from jax.sharding import PartitionSpec as P

CAP = 2
META = 8
VMEM_LIMIT = 20 * 2**20
CHUNKS = 4
SMEM = pltpu.SMEM
VMEM = pltpu.VMEM


def sds(shape, dtype):
    return jax.ShapeDtypeStruct(shape, dtype)


def spec(space=VMEM):
    return pl.BlockSpec(memory_space=space)


def near(x):
    return pltpu.with_memory_space_constraint(x, pltpu.VMEM)


def far(x):
    return pltpu.with_memory_space_constraint(x, pltpu.HBM)


def params():
    return pltpu.CompilerParams(vmem_limit_bytes=VMEM_LIMIT)


def pack(amplitudes, tile_list, owners, local_tiles):
    tiles, width, domain = amplitudes.shape
    rows = CAP * width

    def kernel(list_ref, ids_ref, amp_ref, out_ref, pos_ref, count, amp, meta, load_sem, tile_sem, meta_sem):
        part = tiles // CHUNKS
        loads = []
        for j in range(CHUNKS):
            piece = pl.ds(j * part, part)
            loads.append(pltpu.make_async_copy(amp_ref.at[piece], amp.at[piece], load_sem.at[j]))
            loads[j].start()

        def clear(o, carry):
            count[o] = 0
            return carry

        lax.fori_loop(0, owners, clear, 0, unroll=8)

        def place(t, carry):
            owner = lax.rem(list_ref[0, t], owners)
            rank = count[owner]
            count[owner] = rank + 1
            pos_ref[t] = owner * CAP + rank
            slot = out_ref.at[owner, pl.ds(pl.multiple_of(rank * width, width), width)]
            pltpu.make_async_copy(amp.at[t], slot, tile_sem).start()
            return carry

        ids = ids_ref[...]
        i, k = ids[0:1], ids[1:2]
        owner = jnp.broadcast_to(lax.rem(i, owners).astype(jnp.float32), (tiles, tiles))
        earlier = lax.broadcasted_iota(jnp.int32, (tiles, tiles), 0) < lax.broadcasted_iota(
            jnp.int32, (tiles, tiles), 1
        )
        same = jnp.where((owner == owner.T) & earlier, 1.0, 0.0)
        rank = jnp.sum(same, axis=0, keepdims=True)
        key = lax.div(i, owners) * local_tiles + lax.rem(ids[2:3], local_tiles) + 1
        fields = [v.astype(jnp.float32) for v in (key, lax.div(k, 16), lax.rem(k, 16), ids[3:4])]
        lane = lax.broadcasted_iota(jnp.int32, (domain, tiles), 0)
        row_owner = lax.broadcasted_iota(jnp.int32, (owners * META, tiles), 0) // META
        total = jnp.zeros((owners * META, domain), jnp.float32)
        for c in range(CAP):
            mine = (row_owner.astype(jnp.float32) == owner[0:1]) & (rank == float(c))
            table = jnp.zeros((domain, tiles), jnp.float32)
            for f, value in enumerate(fields):
                table = jnp.where(lane == 4 * c + f, value, table)
            total += lax.dot_general(
                jnp.where(mine, 1.0, 0.0).astype(jnp.bfloat16),
                table.astype(jnp.bfloat16),
                (((1,), (1,)), ((), ())),
                preferred_element_type=jnp.float32,
            )
        meta[...] = total.reshape(owners, META, domain).astype(jnp.bfloat16)
        meta_copy = pltpu.make_async_copy(meta, out_ref.at[:, pl.ds(rows, META)], meta_sem)
        meta_copy.start()
        for j, load in enumerate(loads):
            load.wait()
            lax.fori_loop(j * part, (j + 1) * part, place, 0, unroll=4)
        meta_copy.wait()
        pltpu.make_async_copy(amp, amp_ref, tile_sem).wait()

    return pl.pallas_call(
        kernel,
        out_shape=(pltpu.HBM((owners, rows + META, domain), jnp.bfloat16), sds((tiles,), jnp.int32)),
        in_specs=[spec(SMEM), spec(), spec(pltpu.HBM)],
        out_specs=(spec(pltpu.HBM), spec(SMEM)),
        scratch_shapes=[
            SMEM((owners,), jnp.int32),
            VMEM((tiles, width, domain), jnp.bfloat16),
            VMEM((owners, META, domain), jnp.bfloat16),
            pltpu.SemaphoreType.DMA((CHUNKS,)),
            pltpu.SemaphoreType.DMA,
            pltpu.SemaphoreType.DMA,
        ],
        compiler_params=params(),
        name="pack",
    )(tile_list, tile_list, far(amplitudes))


def owner_core(received, cycle_virtual, cycle_occupied, cycle_core, width, groups):
    sources, message, domain = received.shape
    rank = cycle_core.shape[0]
    rows = CAP * width

    def kernel(got_ref, cv_ref, co_ref, core_ref, out_ref, meta, ids_v, ids, sums, cores, sem, out_sem):
        meta[...] = got_ref[:, rows:, :].astype(jnp.float32).reshape(meta.shape)
        ids_v[...] = meta[pl.ds(0, sources, stride=META), :].astype(jnp.int32)
        ids_copy = pltpu.make_async_copy(ids_v, ids, sem)
        ids_copy.start()
        sums[...] = jnp.zeros_like(sums)
        ids_copy.wait()

        def add(s, carry):
            for c in range(CAP):
                key = ids[s, 4 * c]
                k = ids[s, 4 * c + 1] * 16 + ids[s, 4 * c + 2]
                g = ids[s, 4 * c + 3]
                tile = got_ref[s, c * width : (c + 1) * width, :]
                one = jnp.dot(tile, cv_ref[g], preferred_element_type=jnp.float32)
                sums[key] += one * co_ref[pl.ds(k, 1), :]
            return carry

        lax.fori_loop(0, sources, add, 0, unroll=8)
        grouped = sums[...].astype(jnp.bfloat16).reshape((groups + 1) * width, rank)
        core = jnp.dot(grouped, core_ref[...], preferred_element_type=jnp.float32)
        cores[...] = core.astype(jnp.bfloat16).reshape(cores.shape)

        def answer(s, carry):
            for c in range(CAP):
                slot = out_ref.at[s, pl.ds(c * width, width)]
                pltpu.make_async_copy(cores.at[ids[s, 4 * c]], slot, out_sem).start()
            return carry

        lax.fori_loop(0, sources, answer, 0, unroll=4)
        pltpu.make_async_copy(out_ref, out_ref, out_sem).wait()

    return pl.pallas_call(
        kernel,
        out_shape=pltpu.HBM((sources, rows, rank), jnp.bfloat16),
        in_specs=[spec()] * 4,
        out_specs=spec(pltpu.HBM),
        scratch_shapes=[
            VMEM((sources * META, domain), jnp.float32),
            VMEM((sources, domain), jnp.int32),
            SMEM((sources, domain), jnp.int32),
            VMEM((groups + 1, width, rank), jnp.float32),
            VMEM((groups + 1, width, rank), jnp.bfloat16),
            pltpu.SemaphoreType.DMA,
            pltpu.SemaphoreType.DMA,
        ],
        compiler_params=params(),
        name="owner_core",
    )(near(received), near(cycle_virtual), near(cycle_occupied), near(cycle_core))


def inverse_denominator(tile_list, occ_energy, row_energy, column_energy):
    tiles = tile_list.shape[1]
    local_tiles, width, domain = row_energy.shape

    def kernel(list_ref, occ_ref, re_ref, ce_ref, inv_ref):
        def one(t, carry):
            a = lax.rem(list_ref[2, t], local_tiles)
            occ = occ_ref[list_ref[0, t]] + occ_ref[list_ref[1, t]]
            inv_ref[t] = 1.0 / (re_ref[a] + ce_ref[pl.ds(list_ref[3, t], 1), :] - occ)
            return carry

        lax.fori_loop(0, tiles, one, 0, unroll=4)

    return pl.pallas_call(
        kernel,
        out_shape=sds((tiles, width, domain), jnp.float32),
        in_specs=[spec(SMEM), spec(SMEM)] + [spec()] * 2,
        out_specs=spec(),
        compiler_params=params(),
        name="inverse",
    )(tile_list, occ_energy, row_energy, column_energy)


def ladder_part(tile_list, amplitudes, ladder_virtual, ladder_domain, inverse, cycle_virtual):
    tiles, width, domain = amplitudes.shape
    local_tiles = ladder_virtual.shape[0]
    domains = cycle_virtual.shape[0]

    def kernel(list_ref, amp_ref, lv_ref, ld_ref, inv_ref, cv_ref, base_ref, turned_ref, half):
        def first(t, carry):
            part = jnp.dot(amp_ref[t], ld_ref[list_ref[3, t]], preferred_element_type=jnp.float32)
            half[t] = part.astype(jnp.bfloat16)
            return carry

        lax.fori_loop(0, tiles, first, 0, unroll=8)

        def second(t, carry):
            a = lax.rem(list_ref[2, t], local_tiles)
            ladder = jnp.dot(lv_ref[a], half[t], preferred_element_type=jnp.float32)
            base_ref[t] = amp_ref[t].astype(jnp.float32) + ladder * inv_ref[t]
            return carry

        lax.fori_loop(0, tiles, second, 0, unroll=8)

        def turn(g, carry):
            turned_ref[g] = cv_ref[g].astype(jnp.float32).T.astype(jnp.bfloat16)
            return carry

        lax.fori_loop(0, domains, turn, 0, unroll=2)

    return pl.pallas_call(
        kernel,
        out_shape=(sds(amplitudes.shape, jnp.float32), sds(cycle_virtual.shape, jnp.bfloat16)),
        in_specs=[spec(SMEM)] + [spec()] * 5,
        out_specs=(spec(), spec()),
        scratch_shapes=[VMEM(amplitudes.shape, jnp.bfloat16)],
        compiler_params=params(),
        name="ladder",
    )(tile_list, amplitudes, ladder_virtual, ladder_domain, inverse, cycle_virtual)


def finish(tile_list, position, returned, cycle_turned, cycle_occupied, base, inverse):
    tiles, width, domain = base.shape
    part = tiles // CHUNKS

    def kernel(
        list_ref, pos_ref, ret_ref, cv_ref, co_ref, base_ref, inv_ref, out_ref, base, inv, out, sem, out_sem
    ):
        loads, stores = [], []
        for j in range(CHUNKS):
            piece = pl.ds(j * part, part)
            loads.append(
                (
                    pltpu.make_async_copy(base_ref.at[piece], base.at[piece], sem.at[j, 0]),
                    pltpu.make_async_copy(inv_ref.at[piece], inv.at[piece], sem.at[j, 1]),
                )
            )
            stores.append(pltpu.make_async_copy(out.at[piece], out_ref.at[piece], out_sem.at[j]))

        for pair in loads:
            for copy in pair:
                copy.start()

        def one(t, carry):
            row = pl.multiple_of(lax.rem(pos_ref[t], CAP) * width, width)
            scaled = ret_ref[lax.div(pos_ref[t], CAP), pl.ds(row, width), :].astype(jnp.float32) * co_ref[pl.ds(list_ref[1, t], 1), :]
            term = jnp.dot(scaled.astype(jnp.bfloat16), cv_ref[list_ref[3, t]], preferred_element_type=jnp.float32)
            out[t] = (base[t] + term * inv[t]).astype(jnp.bfloat16)
            return carry

        for j in range(CHUNKS):
            for copy in loads[j]:
                copy.wait()
            lax.fori_loop(j * part, (j + 1) * part, one, 0, unroll=4)
            stores[j].start()
        for copy in stores:
            copy.wait()

    return pl.pallas_call(
        kernel,
        out_shape=sds(base.shape, jnp.bfloat16),
        in_specs=[spec(SMEM), spec(SMEM), spec(), spec(), spec(), spec(pltpu.HBM), spec(pltpu.HBM)],
        out_specs=spec(pltpu.HBM),
        scratch_shapes=[
            VMEM((tiles, width, domain), jnp.float32),
            VMEM((tiles, width, domain), jnp.float32),
            VMEM((tiles, width, domain), jnp.bfloat16),
            pltpu.SemaphoreType.DMA((CHUNKS, 2)),
            pltpu.SemaphoreType.DMA((CHUNKS,)),
        ],
        compiler_params=params(),
        name="finish",
    )(tile_list, position, near(returned), cycle_turned, cycle_occupied, far(base), far(inverse))


def body(
    amplitudes,
    tile_list,
    ladder_virtual_integrals,
    ladder_domain_integrals,
    cycle_virtual,
    cycle_occupied,
    cycle_core,
    occ_energy,
    vir_energy,
):
    tiles, width, domain = amplitudes.shape
    owners = lax.axis_size("occ")
    local_tiles = ladder_virtual_integrals.shape[0]
    groups = -(-occ_energy.shape[0] // owners) * local_tiles
    vir_index = lax.axis_index("vir")
    local_energy = lax.dynamic_slice_in_dim(vir_energy, vir_index * local_tiles * width, local_tiles * width)
    row_energy = jnp.broadcast_to(local_energy.reshape(local_tiles, width, 1), (local_tiles, width, domain))
    column_energy = vir_energy.reshape(-1, domain)

    tile_list = tile_list.T
    cycle_occupied = cycle_occupied.astype(jnp.float32)
    send, position = pack(amplitudes, tile_list, owners, local_tiles)
    received = lax.all_to_all(send, "occ", split_axis=0, concat_axis=0, tiled=True)
    virtual_all = lax.all_gather(cycle_virtual, "vir", axis=0, tiled=True)
    row_energy, _ = lax.optimization_barrier((row_energy, virtual_all))
    inverse = inverse_denominator(tile_list, occ_energy, row_energy, column_energy)
    inverse, virtual_all = lax.optimization_barrier((inverse, virtual_all))
    answers = owner_core(received, virtual_all, cycle_occupied, cycle_core, width, groups)
    returned = lax.all_to_all(answers, "occ", split_axis=0, concat_axis=0, tiled=True)
    domain_own, _ = lax.optimization_barrier((ladder_domain_integrals, virtual_all))
    domain_all = lax.all_gather(domain_own, "vir", axis=0, tiled=True)
    base, turned = ladder_part(
        tile_list, amplitudes, ladder_virtual_integrals, domain_all, inverse, virtual_all
    )
    return finish(tile_list, position, returned, turned, cycle_occupied, base, inverse)


def solution(mesh):
    tile_spec = P(("occ", "vir"), None, None)
    return jax.shard_map(
        body,
        mesh=mesh,
        in_specs=(tile_spec, P(("occ", "vir"), None), P("vir"), P("vir"), P("vir"), P(), P(), P(), P()),
        out_specs=tile_spec,
        check_vma=False,
    )
```

```python
import jax
import jax.numpy as jnp
from jax import lax
from jax.experimental import pallas as pl
from jax.experimental.pallas import tpu as pltpu
from jax.sharding import PartitionSpec as P

CAP = 2
META = 8
VMEM_LIMIT = 20 * 2**20
CHUNKS = 4
PARTS = 2
SMEM = pltpu.SMEM
VMEM = pltpu.VMEM


def sds(shape, dtype):
    return jax.ShapeDtypeStruct(shape, dtype)


def spec(space=VMEM):
    return pl.BlockSpec(memory_space=space)


def near(x):
    return pltpu.with_memory_space_constraint(x, pltpu.VMEM)


def far(x):
    return pltpu.with_memory_space_constraint(x, pltpu.HBM)


def params():
    return pltpu.CompilerParams(vmem_limit_bytes=VMEM_LIMIT)


def pack(amplitudes, tile_list, owners, local_tiles):
    tiles, width, domain = amplitudes.shape
    rows = CAP * width

    def kernel(list_hbm, amp_ref, out_ref, pos_ref, count, list_ref, ids_ref, amp, meta, list_sem, load_sem, tile_sem, meta_sem):
        list_copy = pltpu.make_async_copy(list_hbm, list_ref, list_sem.at[0])
        list_copy.start()
        ids_copy = pltpu.make_async_copy(list_hbm, ids_ref, list_sem.at[1])
        ids_copy.start()
        part = tiles // CHUNKS
        loads = []
        for j in range(CHUNKS):
            piece = pl.ds(j * part, part)
            loads.append(pltpu.make_async_copy(amp_ref.at[piece], amp.at[piece], load_sem.at[j]))
            loads[j].start()

        def clear(o, carry):
            count[o] = 0
            return carry

        lax.fori_loop(0, owners, clear, 0, unroll=8)

        def place(t, carry):
            owner = lax.rem(list_ref[0, t], owners)
            rank = count[owner]
            count[owner] = rank + 1
            pos_ref[t] = owner * CAP + rank
            slot = out_ref.at[owner, pl.ds(pl.multiple_of(rank * width, width), width)]
            pltpu.make_async_copy(amp.at[t], slot, tile_sem).start()
            return carry

        list_copy.wait()
        for j, load in enumerate(loads):
            load.wait()
            lax.fori_loop(j * part, (j + 1) * part, place, 0, unroll=16)
        ids_copy.wait()
        ids = ids_ref[...]
        i, k = ids[0:1], ids[1:2]
        owner = jnp.broadcast_to(lax.rem(i, owners).astype(jnp.float32), (tiles, tiles))
        earlier = lax.broadcasted_iota(jnp.int32, (tiles, tiles), 0) < lax.broadcasted_iota(
            jnp.int32, (tiles, tiles), 1
        )
        same = jnp.where((owner == owner.T) & earlier, 1.0, 0.0)
        rank = jnp.sum(same, axis=0, keepdims=True)
        key = lax.div(i, owners) * local_tiles + lax.rem(ids[2:3], local_tiles) + 1
        fields = [v.astype(jnp.float32) for v in (key, lax.div(k, 16), lax.rem(k, 16), ids[3:4])]
        lane = lax.broadcasted_iota(jnp.int32, (domain, tiles), 0)
        row_owner = lax.broadcasted_iota(jnp.int32, (owners * META, tiles), 0) // META
        total = jnp.zeros((owners * META, domain), jnp.float32)
        for c in range(CAP):
            mine = (row_owner.astype(jnp.float32) == owner[0:1]) & (rank == float(c))
            table = jnp.zeros((domain, tiles), jnp.float32)
            for f, value in enumerate(fields):
                table = jnp.where(lane == 4 * c + f, value, table)
            total += lax.dot_general(
                jnp.where(mine, 1.0, 0.0).astype(jnp.bfloat16),
                table.astype(jnp.bfloat16),
                (((1,), (1,)), ((), ())),
                preferred_element_type=jnp.float32,
            )
        meta[...] = total.reshape(owners, META, domain).astype(jnp.bfloat16)
        meta_copy = pltpu.make_async_copy(meta, out_ref.at[:, pl.ds(rows, META)], meta_sem)
        meta_copy.start()
        meta_copy.wait()
        pltpu.make_async_copy(amp, amp_ref, tile_sem).wait()

    return pl.pallas_call(
        kernel,
        out_shape=(pltpu.HBM((owners, rows + META, domain), jnp.bfloat16), sds((tiles,), jnp.int32)),
        in_specs=[spec(pltpu.HBM), spec(pltpu.HBM)],
        out_specs=(spec(pltpu.HBM), spec(SMEM)),
        scratch_shapes=[
            SMEM((owners,), jnp.int32),
            SMEM(tile_list.shape, jnp.int32),
            VMEM(tile_list.shape, jnp.int32),
            VMEM((tiles, width, domain), jnp.bfloat16),
            VMEM((owners, META, domain), jnp.bfloat16),
            pltpu.SemaphoreType.DMA((2,)),
            pltpu.SemaphoreType.DMA((CHUNKS,)),
            pltpu.SemaphoreType.DMA,
            pltpu.SemaphoreType.DMA,
        ],
        compiler_params=params(),
        name="pack",
    )(far(tile_list), far(amplitudes))


def owner_core(received, cycle_virtual, cycle_occupied, cycle_core, width, groups):
    sources, message, domain = received.shape
    rank = cycle_core.shape[0]
    rows = CAP * width

    part = sources // PARTS

    def kernel(
        got_ref, cv_ref, co_ref, core_ref, out_ref, got, meta_b, meta, ids_v, ids, sums, cores, sem, part_sem, out_sem
    ):
        meta_copy = pltpu.make_async_copy(got_ref.at[:, pl.ds(rows, META)], meta_b, sem)
        meta_copy.start()
        copies = []
        for j in range(PARTS):
            piece = pl.ds(j * part, part)
            copies.append(pltpu.make_async_copy(got_ref.at[piece, pl.ds(0, rows)], got.at[piece], part_sem.at[j]))
            copies[j].start()
        meta_copy.wait()
        meta[...] = meta_b[...].astype(jnp.float32).reshape(meta.shape)
        ids_v[...] = meta[pl.ds(0, sources, stride=META), :].astype(jnp.int32)
        ids_copy = pltpu.make_async_copy(ids_v, ids, sem)
        ids_copy.start()
        sums[...] = jnp.zeros_like(sums)
        ids_copy.wait()

        def add(s, carry):
            for c in range(CAP):
                key = ids[s, 4 * c]
                k = ids[s, 4 * c + 1] * 16 + ids[s, 4 * c + 2]
                g = ids[s, 4 * c + 3]
                tile = got[s, c * width : (c + 1) * width, :]
                one = jnp.dot(tile, cv_ref[g], preferred_element_type=jnp.float32)
                sums[key] += one * co_ref[pl.ds(k, 1), :]
            return carry

        for j, copy in enumerate(copies):
            copy.wait()
            lax.fori_loop(j * part, (j + 1) * part, add, 0, unroll=32)
        grouped = sums[...].astype(jnp.bfloat16).reshape((groups + 1) * width, rank)
        core = jnp.dot(grouped, core_ref[...], preferred_element_type=jnp.float32)
        cores[...] = core.astype(jnp.bfloat16).reshape(cores.shape)

        def answer(s, carry):
            for c in range(CAP):
                slot = out_ref.at[s, pl.ds(c * width, width)]
                pltpu.make_async_copy(cores.at[ids[s, 4 * c]], slot, out_sem).start()
            return carry

        lax.fori_loop(0, sources, answer, 0, unroll=4)
        pltpu.make_async_copy(out_ref, out_ref, out_sem).wait()

    return pl.pallas_call(
        kernel,
        out_shape=pltpu.HBM((sources, rows, rank), jnp.bfloat16),
        in_specs=[spec(pltpu.HBM)] + [spec()] * 3,
        out_specs=spec(pltpu.HBM),
        scratch_shapes=[
            VMEM((sources, rows, domain), jnp.bfloat16),
            VMEM((sources, META, domain), jnp.bfloat16),
            VMEM((sources * META, domain), jnp.float32),
            VMEM((sources, domain), jnp.int32),
            SMEM((sources, domain), jnp.int32),
            VMEM((groups + 1, width, rank), jnp.float32),
            VMEM((groups + 1, width, rank), jnp.bfloat16),
            pltpu.SemaphoreType.DMA,
            pltpu.SemaphoreType.DMA((PARTS,)),
            pltpu.SemaphoreType.DMA,
        ],
        compiler_params=params(),
        name="owner_core",
    )(far(received), near(cycle_virtual), near(cycle_occupied), near(cycle_core))


def inverse_at(t, list_ref, occ_ref, row_ref, column_ref):
    a = lax.rem(list_ref[2, t], row_ref.shape[0])
    occ = occ_ref[list_ref[0, t]] + occ_ref[list_ref[1, t]]
    return 1.0 / (row_ref[a] + column_ref[pl.ds(list_ref[3, t], 1), :] - occ)


def ladder_part(tile_list, amplitudes, ladder_virtual, ladder_domain, energies, cycle_virtual):
    tiles, width, domain = amplitudes.shape
    local_tiles = ladder_virtual.shape[0]
    domains = cycle_virtual.shape[0]

    def kernel(list_ref, occ_ref, amp_ref, lv_ref, ld_ref, row_ref, column_ref, cv_ref, base_ref, turned_ref, half):
        def first(t, carry):
            part = jnp.dot(amp_ref[t], ld_ref[list_ref[3, t]], preferred_element_type=jnp.float32)
            half[t] = part.astype(jnp.bfloat16)
            return carry

        lax.fori_loop(0, tiles, first, 0, unroll=8)

        def second(t, carry):
            a = lax.rem(list_ref[2, t], local_tiles)
            ladder = jnp.dot(lv_ref[a], half[t], preferred_element_type=jnp.float32)
            inverse = inverse_at(t, list_ref, occ_ref, row_ref, column_ref)
            base_ref[t] = amp_ref[t].astype(jnp.float32) + ladder * inverse
            return carry

        lax.fori_loop(0, tiles, second, 0, unroll=8)

        def turn(g, carry):
            turned_ref[g] = cv_ref[g].astype(jnp.float32).T.astype(jnp.bfloat16)
            return carry

        lax.fori_loop(0, domains, turn, 0, unroll=2)

    return pl.pallas_call(
        kernel,
        out_shape=(sds(amplitudes.shape, jnp.float32), sds(cycle_virtual.shape, jnp.bfloat16)),
        in_specs=[spec(SMEM)] * 2 + [spec()] * 6,
        out_specs=(spec(), spec()),
        scratch_shapes=[VMEM(amplitudes.shape, jnp.bfloat16)],
        compiler_params=params(),
        name="ladder",
    )(tile_list, energies[0], amplitudes, ladder_virtual, ladder_domain, energies[1], energies[2], cycle_virtual)


def finish(tile_list, position, returned, cycle_turned, cycle_occupied, base, energies):
    tiles, width, domain = base.shape
    part = tiles // CHUNKS

    def kernel(
        list_ref,
        pos_ref,
        occ_ref,
        row_ref,
        column_ref,
        ret_ref,
        cv_ref,
        co_ref,
        base_ref,
        out_ref,
        core,
        base,
        out,
        sem,
        out_sem,
    ):
        loads, stores = [], []
        for j in range(CHUNKS):
            piece = pl.ds(j * part, part)
            loads.append(pltpu.make_async_copy(base_ref.at[piece], base.at[piece], sem.at[j, 0]))
            stores.append(pltpu.make_async_copy(out.at[piece], out_ref.at[piece], out_sem.at[j]))

        for j in range(CHUNKS):

            def fetch(t, carry):
                slot = pos_ref[t]
                row = pl.multiple_of(lax.rem(slot, CAP) * width, width)
                tile = ret_ref.at[lax.div(slot, CAP), pl.ds(row, width)]
                pltpu.make_async_copy(tile, core.at[t], sem.at[j, 1]).start()
                return carry

            lax.fori_loop(j * part, (j + 1) * part, fetch, 0, unroll=8)
            loads[j].start()

        def one(t, carry):
            scaled = core[t].astype(jnp.float32) * co_ref[pl.ds(list_ref[1, t], 1), :]
            term = jnp.dot(scaled.astype(jnp.bfloat16), cv_ref[list_ref[3, t]], preferred_element_type=jnp.float32)
            inverse = inverse_at(t, list_ref, occ_ref, row_ref, column_ref)
            out[t] = (base[t] + term * inverse).astype(jnp.bfloat16)
            return carry

        for j in range(CHUNKS):
            piece = pl.ds(j * part, part)
            pltpu.make_async_copy(core.at[piece], core.at[piece], sem.at[j, 1]).wait()
            loads[j].wait()
            lax.fori_loop(j * part, (j + 1) * part, one, 0, unroll=16)
            stores[j].start()
        for copy in stores:
            copy.wait()

    return pl.pallas_call(
        kernel,
        out_shape=sds(base.shape, jnp.bfloat16),
        in_specs=[spec(SMEM)] * 3 + [spec()] * 2 + [spec(pltpu.HBM)] + [spec()] * 2 + [spec(pltpu.HBM)],
        out_specs=spec(pltpu.HBM),
        scratch_shapes=[
            VMEM((tiles, width, domain), jnp.bfloat16),
            VMEM((tiles, width, domain), jnp.float32),
            VMEM((tiles, width, domain), jnp.bfloat16),
            pltpu.SemaphoreType.DMA((CHUNKS, 2)),
            pltpu.SemaphoreType.DMA((CHUNKS,)),
        ],
        compiler_params=params(),
        name="finish",
    )(tile_list, position, *energies, far(returned), cycle_turned, cycle_occupied, far(base))


def body(
    amplitudes,
    tile_list,
    ladder_virtual_integrals,
    ladder_domain_integrals,
    cycle_virtual,
    cycle_occupied,
    cycle_core,
    occ_energy,
    vir_energy,
):
    tiles, width, domain = amplitudes.shape
    owners = lax.axis_size("occ")
    local_tiles = ladder_virtual_integrals.shape[0]
    groups = -(-occ_energy.shape[0] // owners) * local_tiles
    vir_index = lax.axis_index("vir")
    local_energy = lax.dynamic_slice_in_dim(vir_energy, vir_index * local_tiles * width, local_tiles * width)
    row_energy = jnp.broadcast_to(local_energy.reshape(local_tiles, width, 1), (local_tiles, width, domain))
    column_energy = vir_energy.reshape(-1, domain)

    tile_list = tile_list.T
    cycle_occupied = cycle_occupied.astype(jnp.float32)
    send, position = pack(amplitudes, tile_list, owners, local_tiles)
    received = lax.all_to_all(send, "occ", split_axis=0, concat_axis=0, tiled=True)
    virtual_all = lax.all_gather(cycle_virtual, "vir", axis=0, tiled=True)
    energies = (occ_energy, row_energy, column_energy)
    answers = owner_core(received, virtual_all, cycle_occupied, cycle_core, width, groups)
    returned = lax.all_to_all(answers, "occ", split_axis=0, concat_axis=0, tiled=True)
    domain_own, _ = lax.optimization_barrier((ladder_domain_integrals, virtual_all))
    domain_all = lax.all_gather(domain_own, "vir", axis=0, tiled=True)
    base, turned = ladder_part(
        tile_list, amplitudes, ladder_virtual_integrals, domain_all, energies, virtual_all
    )
    return finish(tile_list, position, returned, turned, cycle_occupied, base, energies)


def solution(mesh):
    tile_spec = P(("occ", "vir"), None, None)
    return jax.shard_map(
        body,
        mesh=mesh,
        in_specs=(tile_spec, P(("occ", "vir"), None), P("vir"), P("vir"), P("vir"), P(), P(), P(), P()),
        out_specs=tile_spec,
        check_vma=False,
    )
```

```python
import jax
import jax.numpy as jnp
from jax import lax
from jax.experimental import pallas as pl
from jax.experimental.pallas import tpu as pltpu
from jax.sharding import PartitionSpec as P

CAP = 2
META = 8
FIELDS = 4 * CAP
VMEM_LIMIT = 20 * 2**20
CHUNKS = 4
PARTS = 1
SMEM = pltpu.SMEM
VMEM = pltpu.VMEM


def sds(shape, dtype):
    return jax.ShapeDtypeStruct(shape, dtype)


def spec(space=VMEM):
    return pl.BlockSpec(memory_space=space)


def near(x):
    return pltpu.with_memory_space_constraint(x, pltpu.VMEM)


def far(x):
    return pltpu.with_memory_space_constraint(x, pltpu.HBM)


def params():
    return pltpu.CompilerParams(vmem_limit_bytes=VMEM_LIMIT)


def pack(amplitudes, tile_list, owners, local_tiles):
    tiles, width, domain = amplitudes.shape
    rows = CAP * width

    def kernel(list_hbm, amp_ref, out_ref, pos_ref, count, list_ref, ids_ref, amp, meta, list_sem, load_sem, tile_sem, meta_sem):
        list_copy = pltpu.make_async_copy(list_hbm, list_ref, list_sem.at[0])
        list_copy.start()
        ids_copy = pltpu.make_async_copy(list_hbm, ids_ref, list_sem.at[1])
        ids_copy.start()
        part = tiles // CHUNKS
        loads = []
        for j in range(CHUNKS):
            piece = pl.ds(j * part, part)
            loads.append(pltpu.make_async_copy(amp_ref.at[piece], amp.at[piece], load_sem.at[j]))
            loads[j].start()

        def clear(o, carry):
            count[o] = 0
            return carry

        lax.fori_loop(0, owners, clear, 0, unroll=8)

        def place(t, carry):
            owner = lax.rem(list_ref[0, t], owners)
            rank = count[owner]
            count[owner] = rank + 1
            pos_ref[t] = owner * CAP + rank
            slot = out_ref.at[owner, pl.ds(pl.multiple_of(rank * width, width), width)]
            pltpu.make_async_copy(amp.at[t], slot, tile_sem).start()
            return carry

        list_copy.wait()
        for j, load in enumerate(loads):
            load.wait()
            lax.fori_loop(j * part, (j + 1) * part, place, 0, unroll=16)
        ids_copy.wait()
        ids = ids_ref[...]
        i, k = ids[0:1], ids[1:2]
        owner = jnp.broadcast_to(lax.rem(i, owners).astype(jnp.float32), (tiles, tiles))
        earlier = lax.broadcasted_iota(jnp.int32, (tiles, tiles), 0) < lax.broadcasted_iota(
            jnp.int32, (tiles, tiles), 1
        )
        same = jnp.where((owner == owner.T) & earlier, 1.0, 0.0)
        rank = jnp.sum(same, axis=0, keepdims=True)
        key = lax.div(i, owners) * local_tiles + lax.rem(ids[2:3], local_tiles) + 1
        fields = [v.astype(jnp.float32) for v in (key, lax.div(k, 16), lax.rem(k, 16), ids[3:4])]
        lane = lax.broadcasted_iota(jnp.int32, (domain, tiles), 0)
        row_owner = lax.broadcasted_iota(jnp.int32, (owners * META, tiles), 0) // META
        total = jnp.zeros((owners * META, domain), jnp.float32)
        for c in range(CAP):
            mine = (row_owner.astype(jnp.float32) == owner[0:1]) & (rank == float(c))
            table = jnp.zeros((domain, tiles), jnp.float32)
            for f, value in enumerate(fields):
                table = jnp.where(lane == 4 * c + f, value, table)
            total += lax.dot_general(
                jnp.where(mine, 1.0, 0.0).astype(jnp.bfloat16),
                table.astype(jnp.bfloat16),
                (((1,), (1,)), ((), ())),
                preferred_element_type=jnp.float32,
            )
        meta[...] = total.reshape(owners, META, domain).astype(jnp.bfloat16)
        meta_copy = pltpu.make_async_copy(meta, out_ref.at[:, pl.ds(rows, META)], meta_sem)
        meta_copy.start()
        meta_copy.wait()
        pltpu.make_async_copy(amp, amp_ref, tile_sem).wait()

    return pl.pallas_call(
        kernel,
        out_shape=(pltpu.HBM((owners, rows + META, domain), jnp.bfloat16), sds((tiles,), jnp.int32)),
        in_specs=[spec(pltpu.HBM), spec(pltpu.HBM)],
        out_specs=(spec(pltpu.HBM), spec(SMEM)),
        scratch_shapes=[
            SMEM((owners,), jnp.int32),
            SMEM(tile_list.shape, jnp.int32),
            VMEM(tile_list.shape, jnp.int32),
            VMEM((tiles, width, domain), jnp.bfloat16),
            VMEM((owners, META, domain), jnp.bfloat16),
            pltpu.SemaphoreType.DMA((2,)),
            pltpu.SemaphoreType.DMA((CHUNKS,)),
            pltpu.SemaphoreType.DMA,
            pltpu.SemaphoreType.DMA,
        ],
        compiler_params=params(),
        name="pack",
    )(far(tile_list), far(amplitudes))


def owner_core(received, cycle_virtual, cycle_occupied, cycle_core, width, groups):
    sources, message, domain = received.shape
    rank = cycle_core.shape[0]
    rows = CAP * width

    part = sources // PARTS

    def kernel(
        got_ref, cv_ref, co_ref, core_ref, out_ref, got, meta_b, meta, ids_v, ids, sums, cores, sem, part_sem, out_sem
    ):
        meta_copy = pltpu.make_async_copy(got_ref.at[:, pl.ds(rows, META)], meta_b, sem)
        meta_copy.start()
        copies = []
        for j in range(PARTS):
            piece = pl.ds(j * part, part)
            copies.append(pltpu.make_async_copy(got_ref.at[piece, pl.ds(0, rows)], got.at[piece], part_sem.at[j]))
            copies[j].start()
        meta_copy.wait()
        meta[...] = meta_b[...].astype(jnp.float32).reshape(meta.shape)
        turned = meta[pl.ds(0, sources, stride=META), :].T
        ids_v[...] = turned[0:FIELDS].astype(jnp.int32)
        ids_copy = pltpu.make_async_copy(ids_v, ids, sem)
        ids_copy.start()
        sums[...] = jnp.zeros_like(sums)
        ids_copy.wait()

        def add(s, carry):
            for c in range(CAP):
                key = ids[4 * c, s]
                k = ids[4 * c + 1, s] * 16 + ids[4 * c + 2, s]
                g = ids[4 * c + 3, s]
                tile = got[s, c * width : (c + 1) * width, :]
                one = jnp.dot(tile, cv_ref[g], preferred_element_type=jnp.float32)
                sums[key] += one * co_ref[pl.ds(k, 1), :]
            return carry

        for j, copy in enumerate(copies):
            copy.wait()
            lax.fori_loop(j * part, (j + 1) * part, add, 0, unroll=64)
        grouped = sums[...].astype(jnp.bfloat16).reshape((groups + 1) * width, rank)
        core = jnp.dot(grouped, core_ref[...], preferred_element_type=jnp.float32)
        cores[...] = core.astype(jnp.bfloat16).reshape(cores.shape)

        def answer(s, carry):
            for c in range(CAP):
                slot = out_ref.at[s, pl.ds(c * width, width)]
                pltpu.make_async_copy(cores.at[ids[4 * c, s]], slot, out_sem).start()
            return carry

        lax.fori_loop(0, sources, answer, 0, unroll=4)
        pltpu.make_async_copy(out_ref, out_ref, out_sem).wait()

    return pl.pallas_call(
        kernel,
        out_shape=pltpu.HBM((sources, rows, rank), jnp.bfloat16),
        in_specs=[spec(pltpu.HBM)] + [spec()] * 3,
        out_specs=spec(pltpu.HBM),
        scratch_shapes=[
            VMEM((sources, rows, domain), jnp.bfloat16),
            VMEM((sources, META, domain), jnp.bfloat16),
            VMEM((sources * META, domain), jnp.float32),
            VMEM((FIELDS, sources), jnp.int32),
            SMEM((FIELDS, sources), jnp.int32),
            VMEM((groups + 1, width, rank), jnp.float32),
            VMEM((groups + 1, width, rank), jnp.bfloat16),
            pltpu.SemaphoreType.DMA,
            pltpu.SemaphoreType.DMA((PARTS,)),
            pltpu.SemaphoreType.DMA,
        ],
        compiler_params=params(),
        name="owner_core",
    )(far(received), near(cycle_virtual), near(cycle_occupied), near(cycle_core))


def inverse_at(t, list_ref, occ_ref, row_ref, column_ref):
    a = lax.rem(list_ref[2, t], row_ref.shape[0])
    occ = occ_ref[list_ref[0, t]] + occ_ref[list_ref[1, t]]
    return 1.0 / (row_ref[a] + column_ref[pl.ds(list_ref[3, t], 1), :] - occ)


def ladder_part(tile_list, amplitudes, ladder_virtual, ladder_domain, energies, cycle_virtual):
    tiles, width, domain = amplitudes.shape
    local_tiles = ladder_virtual.shape[0]
    domains = cycle_virtual.shape[0]

    def kernel(list_ref, occ_ref, amp_ref, lv_ref, ld_ref, row_ref, column_ref, cv_ref, base_ref, turned_ref, half):
        def first(t, carry):
            part = jnp.dot(amp_ref[t], ld_ref[list_ref[3, t]], preferred_element_type=jnp.float32)
            half[t] = part.astype(jnp.bfloat16)
            return carry

        lax.fori_loop(0, tiles, first, 0, unroll=8)

        def second(t, carry):
            a = lax.rem(list_ref[2, t], local_tiles)
            ladder = jnp.dot(lv_ref[a], half[t], preferred_element_type=jnp.float32)
            inverse = inverse_at(t, list_ref, occ_ref, row_ref, column_ref)
            base_ref[t] = amp_ref[t].astype(jnp.float32) + ladder * inverse
            return carry

        lax.fori_loop(0, tiles, second, 0, unroll=8)

        def turn(g, carry):
            turned_ref[g] = cv_ref[g].astype(jnp.float32).T.astype(jnp.bfloat16)
            return carry

        lax.fori_loop(0, domains, turn, 0, unroll=2)

    return pl.pallas_call(
        kernel,
        out_shape=(sds(amplitudes.shape, jnp.float32), sds(cycle_virtual.shape, jnp.bfloat16)),
        in_specs=[spec(SMEM)] * 2 + [spec()] * 6,
        out_specs=(spec(), spec()),
        scratch_shapes=[VMEM(amplitudes.shape, jnp.bfloat16)],
        compiler_params=params(),
        name="ladder",
    )(tile_list, energies[0], amplitudes, ladder_virtual, ladder_domain, energies[1], energies[2], cycle_virtual)


def finish(tile_list, position, returned, cycle_turned, cycle_occupied, base, energies):
    tiles, width, domain = base.shape
    bounds = [tiles * j // CHUNKS for j in range(CHUNKS + 1)]
    pieces = list(zip(bounds[:-1], bounds[1:]))

    def kernel(
        list_ref,
        pos_ref,
        occ_ref,
        row_ref,
        column_ref,
        ret_ref,
        cv_ref,
        co_ref,
        base_ref,
        out_ref,
        core,
        base,
        out,
        sem,
        out_sem,
    ):
        loads, stores = [], []
        for j, (low, high) in enumerate(pieces):
            piece = pl.ds(low, high - low)
            loads.append(pltpu.make_async_copy(base_ref.at[piece], base.at[piece], sem.at[j, 0]))
            stores.append(pltpu.make_async_copy(out.at[piece], out_ref.at[piece], out_sem.at[j]))

        for j, (low, high) in enumerate(pieces):

            def fetch(t, carry):
                slot = pos_ref[t]
                row = pl.multiple_of(lax.rem(slot, CAP) * width, width)
                tile = ret_ref.at[lax.div(slot, CAP), pl.ds(row, width)]
                pltpu.make_async_copy(tile, core.at[t], sem.at[j, 1]).start()
                return carry

            loads[j].start()
            lax.fori_loop(low, high, fetch, 0, unroll=8)

        def one(t, carry):
            scaled = core[t].astype(jnp.float32) * co_ref[pl.ds(list_ref[1, t], 1), :]
            term = jnp.dot(scaled.astype(jnp.bfloat16), cv_ref[list_ref[3, t]], preferred_element_type=jnp.float32)
            inverse = inverse_at(t, list_ref, occ_ref, row_ref, column_ref)
            out[t] = (base[t] + term * inverse).astype(jnp.bfloat16)
            return carry

        for j, (low, high) in enumerate(pieces):
            piece = pl.ds(low, high - low)
            pltpu.make_async_copy(core.at[piece], core.at[piece], sem.at[j, 1]).wait()
            loads[j].wait()
            lax.fori_loop(low, high, one, 0, unroll=high - low)
            stores[j].start()
        for copy in stores:
            copy.wait()

    return pl.pallas_call(
        kernel,
        out_shape=sds(base.shape, jnp.bfloat16),
        in_specs=[spec(SMEM)] * 3 + [spec()] * 2 + [spec(pltpu.HBM)] + [spec()] * 2 + [spec(pltpu.HBM)],
        out_specs=spec(pltpu.HBM),
        scratch_shapes=[
            VMEM((tiles, width, domain), jnp.bfloat16),
            VMEM((tiles, width, domain), jnp.float32),
            VMEM((tiles, width, domain), jnp.bfloat16),
            pltpu.SemaphoreType.DMA((len(pieces), 2)),
            pltpu.SemaphoreType.DMA((len(pieces),)),
        ],
        compiler_params=params(),
        name="finish",
    )(tile_list, position, *energies, far(returned), cycle_turned, cycle_occupied, far(base))


def body(
    amplitudes,
    tile_list,
    ladder_virtual_integrals,
    ladder_domain_integrals,
    cycle_virtual,
    cycle_occupied,
    cycle_core,
    occ_energy,
    vir_energy,
):
    tiles, width, domain = amplitudes.shape
    owners = lax.axis_size("occ")
    local_tiles = ladder_virtual_integrals.shape[0]
    groups = -(-occ_energy.shape[0] // owners) * local_tiles
    vir_index = lax.axis_index("vir")
    local_energy = lax.dynamic_slice_in_dim(vir_energy, vir_index * local_tiles * width, local_tiles * width)
    row_energy = jnp.broadcast_to(local_energy.reshape(local_tiles, width, 1), (local_tiles, width, domain))
    column_energy = vir_energy.reshape(-1, domain)

    tile_list = tile_list.T
    cycle_occupied = cycle_occupied.astype(jnp.float32)
    send, position = pack(amplitudes, tile_list, owners, local_tiles)
    received = lax.all_to_all(send, "occ", split_axis=0, concat_axis=0, tiled=True)
    virtual_all = lax.all_gather(cycle_virtual, "vir", axis=0, tiled=True)
    energies = (occ_energy, row_energy, column_energy)
    answers = owner_core(received, virtual_all, cycle_occupied, cycle_core, width, groups)
    returned = lax.all_to_all(answers, "occ", split_axis=0, concat_axis=0, tiled=True)
    domain_own, _ = lax.optimization_barrier((ladder_domain_integrals, virtual_all))
    domain_all = lax.all_gather(domain_own, "vir", axis=0, tiled=True)
    base, turned = ladder_part(
        tile_list, amplitudes, ladder_virtual_integrals, domain_all, energies, virtual_all
    )
    return finish(tile_list, position, returned, turned, cycle_occupied, base, energies)


def solution(mesh):
    tile_spec = P(("occ", "vir"), None, None)
    return jax.shard_map(
        body,
        mesh=mesh,
        in_specs=(tile_spec, P(("occ", "vir"), None), P("vir"), P("vir"), P("vir"), P(), P(), P(), P()),
        out_specs=tile_spec,
        check_vma=False,
    )
```

```python
import jax
import jax.numpy as jnp
from jax import lax
from jax.experimental import pallas as pl
from jax.experimental.pallas import tpu as pltpu
from jax.sharding import PartitionSpec as P

CAP = 2
META = 2
FIELDS = 4 * CAP
VMEM_LIMIT = 20 * 2**20
CHUNKS = 4
PARTS = 1
SMEM = pltpu.SMEM
VMEM = pltpu.VMEM


def sds(shape, dtype):
    return jax.ShapeDtypeStruct(shape, dtype)


def spec(space=VMEM):
    return pl.BlockSpec(memory_space=space)


def near(x):
    return pltpu.with_memory_space_constraint(x, pltpu.VMEM)


def far(x):
    return pltpu.with_memory_space_constraint(x, pltpu.HBM)


def params():
    return pltpu.CompilerParams(vmem_limit_bytes=VMEM_LIMIT)


def pack(amplitudes, tile_list, owners, local_tiles):
    tiles, width, domain = amplitudes.shape
    rows = CAP * width

    def kernel(list_hbm, amp_ref, out_ref, pos_ref, count, list_ref, ids_ref, amp, meta, list_sem, load_sem, tile_sem, meta_sem):
        list_copy = pltpu.make_async_copy(list_hbm, list_ref, list_sem.at[0])
        list_copy.start()
        ids_copy = pltpu.make_async_copy(list_hbm, ids_ref, list_sem.at[1])
        ids_copy.start()
        part = tiles // CHUNKS
        loads = []
        for j in range(CHUNKS):
            piece = pl.ds(j * part, part)
            loads.append(pltpu.make_async_copy(amp_ref.at[piece], amp.at[piece], load_sem.at[j]))
            loads[j].start()

        message = out_ref.reshape(owners, rows + META, domain)

        def clear(o, carry):
            count[o] = 0
            return carry

        lax.fori_loop(0, owners, clear, 0, unroll=8)

        def place(t, carry):
            owner = lax.rem(list_ref[0, t], owners)
            rank = count[owner]
            count[owner] = rank + 1
            pos_ref[t] = owner * CAP + rank
            slot = message.at[owner, pl.ds(pl.multiple_of(rank * width, width), width)]
            pltpu.make_async_copy(amp.at[t], slot, tile_sem).start()
            return carry

        list_copy.wait()
        for j, load in enumerate(loads):
            load.wait()
            lax.fori_loop(j * part, (j + 1) * part, place, 0, unroll=16)
        ids_copy.wait()
        ids = ids_ref[...]
        i, k = ids[0:1], ids[1:2]
        owner = jnp.broadcast_to(lax.rem(i, owners).astype(jnp.float32), (tiles, tiles))
        earlier = lax.broadcasted_iota(jnp.int32, (tiles, tiles), 0) < lax.broadcasted_iota(
            jnp.int32, (tiles, tiles), 1
        )
        same = jnp.where((owner == owner.T) & earlier, 1.0, 0.0)
        rank = jnp.sum(same, axis=0, keepdims=True)
        key = lax.div(i, owners) * local_tiles + lax.rem(ids[2:3], local_tiles) + 1
        fields = [v.astype(jnp.float32) for v in (key, lax.div(k, 16), lax.rem(k, 16), ids[3:4])]
        lane = lax.broadcasted_iota(jnp.int32, (domain, tiles), 0)
        row_owner = lax.broadcasted_iota(jnp.int32, (owners * META, tiles), 0) // META
        total = jnp.zeros((owners * META, domain), jnp.float32)
        for c in range(CAP):
            mine = (row_owner.astype(jnp.float32) == owner[0:1]) & (rank == float(c))
            table = jnp.zeros((domain, tiles), jnp.float32)
            for f, value in enumerate(fields):
                table = jnp.where(lane == 4 * c + f, value, table)
            total += lax.dot_general(
                jnp.where(mine, 1.0, 0.0).astype(jnp.bfloat16),
                table.astype(jnp.bfloat16),
                (((1,), (1,)), ((), ())),
                preferred_element_type=jnp.float32,
            )
        meta.reshape(owners * META, domain)[...] = total.astype(jnp.bfloat16)
        meta_copy = pltpu.make_async_copy(meta, out_ref.at[:, pl.ds(rows // META, 1)], meta_sem)
        meta_copy.start()
        meta_copy.wait()
        pltpu.make_async_copy(amp, amp_ref, tile_sem).wait()

    return pl.pallas_call(
        kernel,
        out_shape=(pltpu.HBM((owners, rows // META + 1, META, domain), jnp.bfloat16), sds((tiles,), jnp.int32)),
        in_specs=[spec(pltpu.HBM), spec(pltpu.HBM)],
        out_specs=(spec(pltpu.HBM), spec(SMEM)),
        scratch_shapes=[
            SMEM((owners,), jnp.int32),
            SMEM(tile_list.shape, jnp.int32),
            VMEM(tile_list.shape, jnp.int32),
            VMEM((tiles, width, domain), jnp.bfloat16),
            VMEM((owners, 1, META, domain), jnp.bfloat16),
            pltpu.SemaphoreType.DMA((2,)),
            pltpu.SemaphoreType.DMA((CHUNKS,)),
            pltpu.SemaphoreType.DMA,
            pltpu.SemaphoreType.DMA,
        ],
        compiler_params=params(),
        name="pack",
    )(far(tile_list), far(amplitudes))


def owner_core(received, cycle_virtual, cycle_occupied, cycle_core, width, groups):
    sources, _, _, domain = received.shape
    rank = cycle_core.shape[0]
    rows = CAP * width

    part = sources // PARTS

    def kernel(
        got_ref, cv_ref, co_ref, core_ref, out_ref, got, meta_b, meta, ids_v, ids, sums, cores, sem, part_sem, out_sem
    ):
        message = got_ref.reshape(sources, rows + META, domain)
        meta_copy = pltpu.make_async_copy(got_ref.at[:, pl.ds(rows // META, 1)], meta_b, sem)
        meta_copy.start()
        copies = []
        for j in range(PARTS):
            piece = pl.ds(j * part, part)
            copies.append(pltpu.make_async_copy(message.at[piece, pl.ds(0, rows)], got.at[piece], part_sem.at[j]))
            copies[j].start()
        meta_copy.wait()
        meta[...] = meta_b.reshape(sources * META, domain)[...].astype(jnp.float32)
        turned = meta[pl.ds(0, sources, stride=META), :].T
        ids_v[...] = turned[0:FIELDS].astype(jnp.int32)
        ids_copy = pltpu.make_async_copy(ids_v, ids, sem)
        ids_copy.start()
        sums[...] = jnp.zeros_like(sums)
        ids_copy.wait()

        def add(s, carry):
            for c in range(CAP):
                key = ids[4 * c, s]
                k = ids[4 * c + 1, s] * 16 + ids[4 * c + 2, s]
                g = ids[4 * c + 3, s]
                tile = got[s, c * width : (c + 1) * width, :]
                one = jnp.dot(tile, cv_ref[g], preferred_element_type=jnp.float32)
                sums[key] += one * co_ref[pl.ds(k, 1), :]
            return carry

        for j, copy in enumerate(copies):
            copy.wait()
            lax.fori_loop(j * part, (j + 1) * part, add, 0, unroll=64)
        grouped = sums[...].astype(jnp.bfloat16).reshape((groups + 1) * width, rank)
        core = jnp.dot(grouped, core_ref[...], preferred_element_type=jnp.float32)
        cores[...] = core.astype(jnp.bfloat16).reshape(cores.shape)

        def answer(s, carry):
            for c in range(CAP):
                slot = out_ref.at[s, pl.ds(c * width, width)]
                pltpu.make_async_copy(cores.at[ids[4 * c, s]], slot, out_sem).start()
            return carry

        lax.fori_loop(0, sources, answer, 0, unroll=4)
        pltpu.make_async_copy(out_ref, out_ref, out_sem).wait()

    return pl.pallas_call(
        kernel,
        out_shape=pltpu.HBM((sources, rows, rank), jnp.bfloat16),
        in_specs=[spec(pltpu.HBM)] + [spec()] * 3,
        out_specs=spec(pltpu.HBM),
        scratch_shapes=[
            VMEM((sources, rows, domain), jnp.bfloat16),
            VMEM((sources, 1, META, domain), jnp.bfloat16),
            VMEM((sources * META, domain), jnp.float32),
            VMEM((FIELDS, sources), jnp.int32),
            SMEM((FIELDS, sources), jnp.int32),
            VMEM((groups + 1, width, rank), jnp.float32),
            VMEM((groups + 1, width, rank), jnp.bfloat16),
            pltpu.SemaphoreType.DMA,
            pltpu.SemaphoreType.DMA((PARTS,)),
            pltpu.SemaphoreType.DMA,
        ],
        compiler_params=params(),
        name="owner_core",
    )(far(received), near(cycle_virtual), near(cycle_occupied), near(cycle_core))


def inverse_at(t, list_ref, occ_ref, row_ref, column_ref):
    a = lax.rem(list_ref[2, t], row_ref.shape[0])
    occ = occ_ref[list_ref[0, t]] + occ_ref[list_ref[1, t]]
    return 1.0 / (row_ref[a] + column_ref[pl.ds(list_ref[3, t], 1), :] - occ)


def ladder_part(tile_list, amplitudes, ladder_virtual, ladder_domain, energies, cycle_virtual):
    tiles, width, domain = amplitudes.shape
    local_tiles = ladder_virtual.shape[0]
    domains = cycle_virtual.shape[0]

    def kernel(list_ref, occ_ref, amp_ref, lv_ref, ld_ref, row_ref, column_ref, cv_ref, base_ref, turned_ref, half):
        def first(t, carry):
            part = jnp.dot(amp_ref[t], ld_ref[list_ref[3, t]], preferred_element_type=jnp.float32)
            half[t] = part.astype(jnp.bfloat16)
            return carry

        lax.fori_loop(0, tiles, first, 0, unroll=8)

        def second(t, carry):
            a = lax.rem(list_ref[2, t], local_tiles)
            ladder = jnp.dot(lv_ref[a], half[t], preferred_element_type=jnp.float32)
            inverse = inverse_at(t, list_ref, occ_ref, row_ref, column_ref)
            base_ref[t] = amp_ref[t].astype(jnp.float32) + ladder * inverse
            return carry

        lax.fori_loop(0, tiles, second, 0, unroll=8)

        def turn(g, carry):
            turned_ref[g] = cv_ref[g].astype(jnp.float32).T.astype(jnp.bfloat16)
            return carry

        lax.fori_loop(0, domains, turn, 0, unroll=2)

    return pl.pallas_call(
        kernel,
        out_shape=(sds(amplitudes.shape, jnp.float32), sds(cycle_virtual.shape, jnp.bfloat16)),
        in_specs=[spec(SMEM)] * 2 + [spec()] * 6,
        out_specs=(spec(), spec()),
        scratch_shapes=[VMEM(amplitudes.shape, jnp.bfloat16)],
        compiler_params=params(),
        name="ladder",
    )(tile_list, energies[0], amplitudes, ladder_virtual, ladder_domain, energies[1], energies[2], cycle_virtual)


def finish(tile_list, position, returned, cycle_turned, cycle_occupied, base, energies):
    tiles, width, domain = base.shape
    bounds = [tiles * j // CHUNKS for j in range(CHUNKS + 1)]
    pieces = list(zip(bounds[:-1], bounds[1:]))

    def kernel(
        list_ref,
        pos_ref,
        occ_ref,
        row_ref,
        column_ref,
        ret_ref,
        cv_ref,
        co_ref,
        base_ref,
        out_ref,
        core,
        base,
        out,
        sem,
        out_sem,
    ):
        loads, stores = [], []
        for j, (low, high) in enumerate(pieces):
            piece = pl.ds(low, high - low)
            loads.append(pltpu.make_async_copy(base_ref.at[piece], base.at[piece], sem.at[j, 0]))
            stores.append(pltpu.make_async_copy(out.at[piece], out_ref.at[piece], out_sem.at[j]))

        for j, (low, high) in enumerate(pieces):

            def fetch(t, carry):
                slot = pos_ref[t]
                row = pl.multiple_of(lax.rem(slot, CAP) * width, width)
                tile = ret_ref.at[lax.div(slot, CAP), pl.ds(row, width)]
                pltpu.make_async_copy(tile, core.at[t], sem.at[j, 1]).start()
                return carry

            loads[j].start()
            lax.fori_loop(low, high, fetch, 0, unroll=8)

        def one(t, carry):
            scaled = core[t].astype(jnp.float32) * co_ref[pl.ds(list_ref[1, t], 1), :]
            term = jnp.dot(scaled.astype(jnp.bfloat16), cv_ref[list_ref[3, t]], preferred_element_type=jnp.float32)
            inverse = inverse_at(t, list_ref, occ_ref, row_ref, column_ref)
            out[t] = (base[t] + term * inverse).astype(jnp.bfloat16)
            return carry

        for j, (low, high) in enumerate(pieces):
            piece = pl.ds(low, high - low)
            pltpu.make_async_copy(core.at[piece], core.at[piece], sem.at[j, 1]).wait()
            loads[j].wait()
            lax.fori_loop(low, high, one, 0, unroll=high - low)
            stores[j].start()
        for copy in stores:
            copy.wait()

    return pl.pallas_call(
        kernel,
        out_shape=sds(base.shape, jnp.bfloat16),
        in_specs=[spec(SMEM)] * 3 + [spec()] * 2 + [spec(pltpu.HBM)] + [spec()] * 2 + [spec(pltpu.HBM)],
        out_specs=spec(pltpu.HBM),
        scratch_shapes=[
            VMEM((tiles, width, domain), jnp.bfloat16),
            VMEM((tiles, width, domain), jnp.float32),
            VMEM((tiles, width, domain), jnp.bfloat16),
            pltpu.SemaphoreType.DMA((len(pieces), 2)),
            pltpu.SemaphoreType.DMA((len(pieces),)),
        ],
        compiler_params=params(),
        name="finish",
    )(tile_list, position, *energies, far(returned), cycle_turned, cycle_occupied, far(base))


def body(
    amplitudes,
    tile_list,
    ladder_virtual_integrals,
    ladder_domain_integrals,
    cycle_virtual,
    cycle_occupied,
    cycle_core,
    occ_energy,
    vir_energy,
):
    tiles, width, domain = amplitudes.shape
    owners = lax.axis_size("occ")
    local_tiles = ladder_virtual_integrals.shape[0]
    groups = -(-occ_energy.shape[0] // owners) * local_tiles
    vir_index = lax.axis_index("vir")
    local_energy = lax.dynamic_slice_in_dim(vir_energy, vir_index * local_tiles * width, local_tiles * width)
    row_energy = jnp.broadcast_to(local_energy.reshape(local_tiles, width, 1), (local_tiles, width, domain))
    column_energy = vir_energy.reshape(-1, domain)

    tile_list = tile_list.T
    cycle_occupied = cycle_occupied.astype(jnp.float32)
    send, position = pack(amplitudes, tile_list, owners, local_tiles)
    received = lax.all_to_all(send, "occ", split_axis=0, concat_axis=0, tiled=True)
    virtual_all = lax.all_gather(cycle_virtual, "vir", axis=0, tiled=True)
    energies = (occ_energy, row_energy, column_energy)
    answers = owner_core(received, virtual_all, cycle_occupied, cycle_core, width, groups)
    returned = lax.all_to_all(answers, "occ", split_axis=0, concat_axis=0, tiled=True)
    domain_own, _ = lax.optimization_barrier((ladder_domain_integrals, virtual_all))
    domain_all = lax.all_gather(domain_own, "vir", axis=0, tiled=True)
    base, turned = ladder_part(
        tile_list, amplitudes, ladder_virtual_integrals, domain_all, energies, virtual_all
    )
    return finish(tile_list, position, returned, turned, cycle_occupied, base, energies)


def solution(mesh):
    tile_spec = P(("occ", "vir"), None, None)
    return jax.shard_map(
        body,
        mesh=mesh,
        in_specs=(tile_spec, P(("occ", "vir"), None), P("vir"), P("vir"), P("vir"), P(), P(), P(), P()),
        out_specs=tile_spec,
        check_vma=False,
    )
```

```python
import jax
import jax.numpy as jnp
from jax import lax
from jax.experimental import pallas as pl
from jax.experimental.pallas import tpu as pltpu
from jax.sharding import PartitionSpec as P

CAP = 2
META = 2
FIELDS = 4 * CAP
VMEM_LIMIT = 20 * 2**20
CHUNKS = 4
SMEM = pltpu.SMEM
VMEM = pltpu.VMEM


def sds(shape, dtype):
    return jax.ShapeDtypeStruct(shape, dtype)


def spec(space=VMEM):
    return pl.BlockSpec(memory_space=space)


def near(x):
    return pltpu.with_memory_space_constraint(x, pltpu.VMEM)


def far(x):
    return pltpu.with_memory_space_constraint(x, pltpu.HBM)


def params():
    return pltpu.CompilerParams(vmem_limit_bytes=VMEM_LIMIT)


def pack(amplitudes, tile_list, owners, local_tiles):
    tiles, width, domain = amplitudes.shape
    rows = CAP * width

    def kernel(list_hbm, amp_ref, out_ref, pos_ref, count, list_ref, ids_ref, amp, meta, list_sem, load_sem, tile_sem, meta_sem):
        list_copy = pltpu.make_async_copy(list_hbm, list_ref, list_sem.at[0])
        list_copy.start()
        ids_copy = pltpu.make_async_copy(list_hbm, ids_ref, list_sem.at[1])
        ids_copy.start()
        part = tiles // CHUNKS
        loads = []
        for j in range(CHUNKS):
            piece = pl.ds(j * part, part)
            loads.append(pltpu.make_async_copy(amp_ref.at[piece], amp.at[piece], load_sem.at[j]))
            loads[j].start()

        message = out_ref.reshape(owners, rows + META, domain)

        def clear(o, carry):
            count[o] = 0
            return carry

        lax.fori_loop(0, owners, clear, 0, unroll=8)

        def place(t, carry):
            owner = lax.rem(list_ref[0, t], owners)
            rank = count[owner]
            count[owner] = rank + 1
            pos_ref[t] = owner * CAP + rank
            slot = message.at[owner, pl.ds(pl.multiple_of(rank * width, width), width)]
            pltpu.make_async_copy(amp.at[t], slot, tile_sem).start()
            return carry

        list_copy.wait()
        for j, load in enumerate(loads):
            load.wait()
            lax.fori_loop(j * part, (j + 1) * part, place, 0, unroll=16)
        ids_copy.wait()
        ids = ids_ref[...]
        i, k = ids[0:1], ids[1:2]
        owner = jnp.broadcast_to(lax.rem(i, owners).astype(jnp.float32), (tiles, tiles))
        earlier = lax.broadcasted_iota(jnp.int32, (tiles, tiles), 0) < lax.broadcasted_iota(
            jnp.int32, (tiles, tiles), 1
        )
        same = jnp.where((owner == owner.T) & earlier, 1.0, 0.0)
        rank = jnp.sum(same, axis=0, keepdims=True)
        key = lax.div(i, owners) * local_tiles + lax.rem(ids[2:3], local_tiles) + 1
        fields = [v.astype(jnp.float32) for v in (key, lax.div(k, 16), lax.rem(k, 16), ids[3:4])]
        lane = lax.broadcasted_iota(jnp.int32, (domain, tiles), 0)
        row_owner = lax.broadcasted_iota(jnp.int32, (owners * META, tiles), 0) // META
        total = jnp.zeros((owners * META, domain), jnp.float32)
        for c in range(CAP):
            mine = (row_owner.astype(jnp.float32) == owner[0:1]) & (rank == float(c))
            table = jnp.zeros((domain, tiles), jnp.float32)
            for f, value in enumerate(fields):
                table = jnp.where(lane == 4 * c + f, value, table)
            total += lax.dot_general(
                jnp.where(mine, 1.0, 0.0).astype(jnp.bfloat16),
                table.astype(jnp.bfloat16),
                (((1,), (1,)), ((), ())),
                preferred_element_type=jnp.float32,
            )
        meta.reshape(owners * META, domain)[...] = total.astype(jnp.bfloat16)
        meta_copy = pltpu.make_async_copy(meta, out_ref.at[:, pl.ds(rows // META, 1)], meta_sem)
        meta_copy.start()
        meta_copy.wait()
        pltpu.make_async_copy(amp, amp_ref, tile_sem).wait()

    return pl.pallas_call(
        kernel,
        out_shape=(pltpu.HBM((owners, rows // META + 1, META, domain), jnp.bfloat16), sds((tiles,), jnp.int32)),
        in_specs=[spec(pltpu.HBM), spec(pltpu.HBM)],
        out_specs=(spec(pltpu.HBM), spec(SMEM)),
        scratch_shapes=[
            SMEM((owners,), jnp.int32),
            SMEM(tile_list.shape, jnp.int32),
            VMEM(tile_list.shape, jnp.int32),
            VMEM((tiles, width, domain), jnp.bfloat16),
            VMEM((owners, 1, META, domain), jnp.bfloat16),
            pltpu.SemaphoreType.DMA((2,)),
            pltpu.SemaphoreType.DMA((CHUNKS,)),
            pltpu.SemaphoreType.DMA,
            pltpu.SemaphoreType.DMA,
        ],
        compiler_params=params(),
        name="pack",
    )(far(tile_list), far(amplitudes))


def owner_core(received, cycle_virtual, cycle_occupied, cycle_core, width, groups):
    sources, _, _, domain = received.shape
    rank = cycle_core.shape[0]
    rows = CAP * width

    def kernel(got_ref, cv_ref, co_ref, core_ref, out_ref, meta, ids_v, ids, sums, cores, sem, out_sem):
        got = got_ref.reshape(sources, rows + META, domain)
        meta[...] = got_ref[:, rows // META, 0, :].astype(jnp.float32)
        ids_v[...] = meta[...].T[0:FIELDS].astype(jnp.int32)
        ids_copy = pltpu.make_async_copy(ids_v, ids, sem)
        ids_copy.start()
        sums[...] = jnp.zeros_like(sums)
        ids_copy.wait()

        def add(s, carry):
            for c in range(CAP):
                key = ids[4 * c, s]
                k = ids[4 * c + 1, s] * 16 + ids[4 * c + 2, s]
                g = ids[4 * c + 3, s]
                tile = got[s, c * width : (c + 1) * width, :]
                one = jnp.dot(tile, cv_ref[g], preferred_element_type=jnp.float32)
                sums[key] += one * co_ref[pl.ds(k, 1), :]
            return carry

        lax.fori_loop(0, sources, add, 0, unroll=64)
        grouped = sums[...].astype(jnp.bfloat16).reshape((groups + 1) * width, rank)
        core = jnp.dot(grouped, core_ref[...], preferred_element_type=jnp.float32)
        cores[...] = core.astype(jnp.bfloat16).reshape(cores.shape)

        def answer(s, carry):
            for c in range(CAP):
                slot = out_ref.at[s, pl.ds(c * width, width)]
                pltpu.make_async_copy(cores.at[ids[4 * c, s]], slot, out_sem).start()
            return carry

        lax.fori_loop(0, sources, answer, 0, unroll=4)
        pltpu.make_async_copy(out_ref, out_ref, out_sem).wait()

    return pl.pallas_call(
        kernel,
        out_shape=pltpu.HBM((sources, rows, rank), jnp.bfloat16),
        in_specs=[spec()] * 4,
        out_specs=spec(pltpu.HBM),
        scratch_shapes=[
            VMEM((sources, domain), jnp.float32),
            VMEM((FIELDS, sources), jnp.int32),
            SMEM((FIELDS, sources), jnp.int32),
            VMEM((groups + 1, width, rank), jnp.float32),
            VMEM((groups + 1, width, rank), jnp.bfloat16),
            pltpu.SemaphoreType.DMA,
            pltpu.SemaphoreType.DMA,
        ],
        compiler_params=params(),
        name="owner_core",
    )(near(received), near(cycle_virtual), near(cycle_occupied), near(cycle_core))


def inverse_at(t, list_ref, occ_ref, row_ref, column_ref):
    a = lax.rem(list_ref[2, t], row_ref.shape[0])
    occ = occ_ref[list_ref[0, t]] + occ_ref[list_ref[1, t]]
    return 1.0 / (row_ref[a] + column_ref[pl.ds(list_ref[3, t], 1), :] - occ)


def ladder_part(tile_list, amplitudes, ladder_virtual, ladder_domain, energies, cycle_virtual):
    tiles, width, domain = amplitudes.shape
    local_tiles = ladder_virtual.shape[0]
    domains = cycle_virtual.shape[0]

    def kernel(list_ref, occ_ref, amp_ref, lv_ref, ld_ref, row_ref, column_ref, cv_ref, base_ref, turned_ref, half):
        def first(t, carry):
            part = jnp.dot(amp_ref[t], ld_ref[list_ref[3, t]], preferred_element_type=jnp.float32)
            half[t] = part.astype(jnp.bfloat16)
            return carry

        lax.fori_loop(0, tiles, first, 0, unroll=8)

        def second(t, carry):
            a = lax.rem(list_ref[2, t], local_tiles)
            ladder = jnp.dot(lv_ref[a], half[t], preferred_element_type=jnp.float32)
            inverse = inverse_at(t, list_ref, occ_ref, row_ref, column_ref)
            base_ref[t] = amp_ref[t].astype(jnp.float32) + ladder * inverse
            return carry

        lax.fori_loop(0, tiles, second, 0, unroll=8)

        def turn(g, carry):
            turned_ref[g] = cv_ref[g].astype(jnp.float32).T.astype(jnp.bfloat16)
            return carry

        lax.fori_loop(0, domains, turn, 0, unroll=2)

    return pl.pallas_call(
        kernel,
        out_shape=(sds(amplitudes.shape, jnp.float32), sds(cycle_virtual.shape, jnp.bfloat16)),
        in_specs=[spec(SMEM)] * 2 + [spec()] * 6,
        out_specs=(spec(), spec()),
        scratch_shapes=[VMEM(amplitudes.shape, jnp.bfloat16)],
        compiler_params=params(),
        name="ladder",
    )(tile_list, energies[0], amplitudes, ladder_virtual, ladder_domain, energies[1], energies[2], cycle_virtual)


def finish(tile_list, position, returned, cycle_turned, cycle_occupied, base, energies):
    tiles, width, domain = base.shape
    bounds = [tiles * j // CHUNKS for j in range(CHUNKS + 1)]
    pieces = list(zip(bounds[:-1], bounds[1:]))

    def kernel(
        list_ref,
        pos_ref,
        occ_ref,
        row_ref,
        column_ref,
        ret_ref,
        cv_ref,
        co_ref,
        base_ref,
        out_ref,
        core,
        base,
        out,
        sem,
        out_sem,
    ):
        loads, stores = [], []
        for j, (low, high) in enumerate(pieces):
            piece = pl.ds(low, high - low)
            loads.append(pltpu.make_async_copy(base_ref.at[piece], base.at[piece], sem.at[j, 0]))
            stores.append(pltpu.make_async_copy(out.at[piece], out_ref.at[piece], out_sem.at[j]))

        for j, (low, high) in enumerate(pieces):

            def fetch(t, carry):
                slot = pos_ref[t]
                row = pl.multiple_of(lax.rem(slot, CAP) * width, width)
                tile = ret_ref.at[lax.div(slot, CAP), pl.ds(row, width)]
                pltpu.make_async_copy(tile, core.at[t], sem.at[j, 1]).start()
                return carry

            loads[j].start()
            lax.fori_loop(low, high, fetch, 0, unroll=8)

        def one(t, carry):
            scaled = core[t].astype(jnp.float32) * co_ref[pl.ds(list_ref[1, t], 1), :]
            term = jnp.dot(scaled.astype(jnp.bfloat16), cv_ref[list_ref[3, t]], preferred_element_type=jnp.float32)
            inverse = inverse_at(t, list_ref, occ_ref, row_ref, column_ref)
            out[t] = (base[t] + term * inverse).astype(jnp.bfloat16)
            return carry

        for j, (low, high) in enumerate(pieces):
            piece = pl.ds(low, high - low)
            pltpu.make_async_copy(core.at[piece], core.at[piece], sem.at[j, 1]).wait()
            loads[j].wait()
            lax.fori_loop(low, high, one, 0, unroll=high - low)
            stores[j].start()
        for copy in stores:
            copy.wait()

    return pl.pallas_call(
        kernel,
        out_shape=sds(base.shape, jnp.bfloat16),
        in_specs=[spec(SMEM)] * 3 + [spec()] * 2 + [spec(pltpu.HBM)] + [spec()] * 2 + [spec(pltpu.HBM)],
        out_specs=spec(pltpu.HBM),
        scratch_shapes=[
            VMEM((tiles, width, domain), jnp.bfloat16),
            VMEM((tiles, width, domain), jnp.float32),
            VMEM((tiles, width, domain), jnp.bfloat16),
            pltpu.SemaphoreType.DMA((len(pieces), 2)),
            pltpu.SemaphoreType.DMA((len(pieces),)),
        ],
        compiler_params=params(),
        name="finish",
    )(tile_list, position, *energies, far(returned), cycle_turned, cycle_occupied, far(base))


def body(
    amplitudes,
    tile_list,
    ladder_virtual_integrals,
    ladder_domain_integrals,
    cycle_virtual,
    cycle_occupied,
    cycle_core,
    occ_energy,
    vir_energy,
):
    tiles, width, domain = amplitudes.shape
    owners = lax.axis_size("occ")
    local_tiles = ladder_virtual_integrals.shape[0]
    groups = -(-occ_energy.shape[0] // owners) * local_tiles
    vir_index = lax.axis_index("vir")
    local_energy = lax.dynamic_slice_in_dim(vir_energy, vir_index * local_tiles * width, local_tiles * width)
    row_energy = jnp.broadcast_to(local_energy.reshape(local_tiles, width, 1), (local_tiles, width, domain))
    column_energy = vir_energy.reshape(-1, domain)

    tile_list = tile_list.T
    cycle_occupied = cycle_occupied.astype(jnp.float32)
    send, position = pack(amplitudes, tile_list, owners, local_tiles)
    received = lax.all_to_all(send, "occ", split_axis=0, concat_axis=0, tiled=True)
    virtual_all = lax.all_gather(cycle_virtual, "vir", axis=0, tiled=True)
    energies = (occ_energy, row_energy, column_energy)
    answers = owner_core(received, virtual_all, cycle_occupied, cycle_core, width, groups)
    returned = lax.all_to_all(answers, "occ", split_axis=0, concat_axis=0, tiled=True)
    domain_own, _ = lax.optimization_barrier((ladder_domain_integrals, virtual_all))
    domain_all = lax.all_gather(domain_own, "vir", axis=0, tiled=True)
    base, turned = ladder_part(
        tile_list, amplitudes, ladder_virtual_integrals, domain_all, energies, virtual_all
    )
    return finish(tile_list, position, returned, turned, cycle_occupied, base, energies)


def solution(mesh):
    tile_spec = P(("occ", "vir"), None, None)
    return jax.shard_map(
        body,
        mesh=mesh,
        in_specs=(tile_spec, P(("occ", "vir"), None), P("vir"), P("vir"), P("vir"), P(), P(), P(), P()),
        out_specs=tile_spec,
        check_vma=False,
    )
```

```python
import jax
import jax.numpy as jnp
from jax import lax
from jax.experimental import pallas as pl
from jax.experimental.pallas import tpu as pltpu
from jax.sharding import PartitionSpec as P

CAP = 2
META = 2
FIELDS = 4 * CAP
VMEM_LIMIT = 20 * 2**20
CHUNKS = 4
SMEM = pltpu.SMEM
VMEM = pltpu.VMEM


def sds(shape, dtype):
    return jax.ShapeDtypeStruct(shape, dtype)


def spec(space=VMEM):
    return pl.BlockSpec(memory_space=space)


def near(x):
    return pltpu.with_memory_space_constraint(x, pltpu.VMEM)


def far(x):
    return pltpu.with_memory_space_constraint(x, pltpu.HBM)


def params():
    return pltpu.CompilerParams(vmem_limit_bytes=VMEM_LIMIT)


def pack(amplitudes, tile_list, owners, local_tiles):
    tiles, width, domain = amplitudes.shape
    rows = CAP * width

    def kernel(list_hbm, amp_ref, out_ref, pos_ref, count, list_ref, ids_ref, amp, meta, list_sem, load_sem, tile_sem, meta_sem):
        list_copy = pltpu.make_async_copy(list_hbm, list_ref, list_sem.at[0])
        list_copy.start()
        ids_copy = pltpu.make_async_copy(list_hbm, ids_ref, list_sem.at[1])
        ids_copy.start()
        part = tiles // CHUNKS
        loads = []
        for j in range(CHUNKS):
            piece = pl.ds(j * part, part)
            loads.append(pltpu.make_async_copy(amp_ref.at[piece], amp.at[piece], load_sem.at[j]))
            loads[j].start()

        message = out_ref.reshape(owners, rows + META, domain)

        def clear(o, carry):
            count[o] = 0
            return carry

        lax.fori_loop(0, owners, clear, 0, unroll=8)

        def place(t, carry):
            owner = lax.rem(list_ref[0, t], owners)
            rank = count[owner]
            count[owner] = rank + 1
            pos_ref[t] = owner * CAP + rank
            slot = message.at[owner, pl.ds(pl.multiple_of(rank * width, width), width)]
            pltpu.make_async_copy(amp.at[t], slot, tile_sem).start()
            return carry

        list_copy.wait()
        for j, load in enumerate(loads):
            load.wait()
            lax.fori_loop(j * part, (j + 1) * part, place, 0, unroll=16)
        ids_copy.wait()
        ids = ids_ref[...]
        i, k = ids[0:1], ids[1:2]
        owner = jnp.broadcast_to(lax.rem(i, owners).astype(jnp.float32), (tiles, tiles))
        earlier = lax.broadcasted_iota(jnp.int32, (tiles, tiles), 0) < lax.broadcasted_iota(
            jnp.int32, (tiles, tiles), 1
        )
        same = jnp.where((owner == owner.T) & earlier, 1.0, 0.0)
        rank = jnp.sum(same, axis=0, keepdims=True)
        key = lax.div(i, owners) * local_tiles + lax.rem(ids[2:3], local_tiles) + 1
        fields = [v.astype(jnp.float32) for v in (key, lax.div(k, 16), lax.rem(k, 16), ids[3:4])]
        lane = lax.broadcasted_iota(jnp.int32, (domain, tiles), 0)
        row_owner = lax.broadcasted_iota(jnp.int32, (owners * META, tiles), 0) // META
        total = jnp.zeros((owners * META, domain), jnp.float32)
        for c in range(CAP):
            mine = (row_owner.astype(jnp.float32) == owner[0:1]) & (rank == float(c))
            table = jnp.zeros((domain, tiles), jnp.float32)
            for f, value in enumerate(fields):
                table = jnp.where(lane == 4 * c + f, value, table)
            total += lax.dot_general(
                jnp.where(mine, 1.0, 0.0).astype(jnp.bfloat16),
                table.astype(jnp.bfloat16),
                (((1,), (1,)), ((), ())),
                preferred_element_type=jnp.float32,
            )
        meta.reshape(owners * META, domain)[...] = total.astype(jnp.bfloat16)
        meta_copy = pltpu.make_async_copy(meta, out_ref.at[:, pl.ds(rows // META, 1)], meta_sem)
        meta_copy.start()
        meta_copy.wait()
        pltpu.make_async_copy(amp, amp_ref, tile_sem).wait()

    return pl.pallas_call(
        kernel,
        out_shape=(pltpu.HBM((owners, rows // META + 1, META, domain), jnp.bfloat16), sds((tiles,), jnp.int32)),
        in_specs=[spec(pltpu.HBM), spec(pltpu.HBM)],
        out_specs=(spec(pltpu.HBM), spec(SMEM)),
        scratch_shapes=[
            SMEM((owners,), jnp.int32),
            SMEM(tile_list.shape, jnp.int32),
            VMEM(tile_list.shape, jnp.int32),
            VMEM((tiles, width, domain), jnp.bfloat16),
            VMEM((owners, 1, META, domain), jnp.bfloat16),
            pltpu.SemaphoreType.DMA((2,)),
            pltpu.SemaphoreType.DMA((CHUNKS,)),
            pltpu.SemaphoreType.DMA,
            pltpu.SemaphoreType.DMA,
        ],
        compiler_params=params(),
        name="pack",
    )(far(tile_list), far(amplitudes))


def owner_core(received, cycle_virtual, cycle_occupied, cycle_core, width, groups):
    sources, _, _, domain = received.shape
    rank = cycle_core.shape[0]
    rows = CAP * width

    def kernel(got_ref, cv_ref, co_ref, core_ref, out_ref, meta, ids_v, ids, sums, cores, sem, out_sem):
        got = got_ref.reshape(sources, rows + META, domain)
        meta[...] = got_ref[:, rows // META, 0, :].astype(jnp.float32)
        ids_v[...] = meta[...].T[0:FIELDS].astype(jnp.int32)
        ids_copy = pltpu.make_async_copy(ids_v, ids, sem)
        ids_copy.start()
        sums[...] = jnp.zeros_like(sums)
        ids_copy.wait()

        def add(s, carry):
            for c in range(CAP):
                key = ids[4 * c, s]
                k = ids[4 * c + 1, s] * 16 + ids[4 * c + 2, s]
                g = ids[4 * c + 3, s]
                tile = got[s, c * width : (c + 1) * width, :]
                one = jnp.dot(tile, cv_ref[g], preferred_element_type=jnp.float32)
                sums[key] += one * co_ref[pl.ds(k, 1), :]
            return carry

        lax.fori_loop(0, sources, add, 0, unroll=64)
        grouped = sums[...].astype(jnp.bfloat16).reshape((groups + 1) * width, rank)
        core = jnp.dot(grouped, core_ref[...], preferred_element_type=jnp.float32)
        cores[...] = core.astype(jnp.bfloat16).reshape(cores.shape)

        def answer(s, carry):
            for c in range(CAP):
                slot = out_ref.at[s, pl.ds(c * width, width)]
                pltpu.make_async_copy(cores.at[ids[4 * c, s]], slot, out_sem).start()
            return carry

        lax.fori_loop(0, sources, answer, 0, unroll=4)
        pltpu.make_async_copy(out_ref, out_ref, out_sem).wait()

    return pl.pallas_call(
        kernel,
        out_shape=pltpu.HBM((sources, rows, rank), jnp.bfloat16),
        in_specs=[spec()] * 4,
        out_specs=spec(pltpu.HBM),
        scratch_shapes=[
            VMEM((sources, domain), jnp.float32),
            VMEM((FIELDS, sources), jnp.int32),
            SMEM((FIELDS, sources), jnp.int32),
            VMEM((groups + 1, width, rank), jnp.float32),
            VMEM((groups + 1, width, rank), jnp.bfloat16),
            pltpu.SemaphoreType.DMA,
            pltpu.SemaphoreType.DMA,
        ],
        compiler_params=params(),
        name="owner_core",
    )(near(received), near(cycle_virtual), near(cycle_occupied), near(cycle_core))


def inverse_at(t, list_ref, occ_ref, row_ref, column_ref):
    a = lax.rem(list_ref[2, t], row_ref.shape[0])
    occ = occ_ref[list_ref[0, t]] + occ_ref[list_ref[1, t]]
    return 1.0 / (row_ref[a] + column_ref[pl.ds(list_ref[3, t], 1), :] - occ)


def ladder_part(tile_list, amplitudes, ladder_virtual, ladder_domain, energies, cycle_virtual):
    tiles, width, domain = amplitudes.shape
    local_tiles = ladder_virtual.shape[0]
    domains = cycle_virtual.shape[0]

    def kernel(list_ref, occ_ref, amp_ref, lv_ref, ld_ref, row_ref, column_ref, cv_ref, base_ref, turned_ref, half):
        def first(t, carry):
            part = jnp.dot(amp_ref[t], ld_ref[list_ref[3, t]], preferred_element_type=jnp.float32)
            half[t] = part.astype(jnp.bfloat16)
            return carry

        lax.fori_loop(0, tiles, first, 0, unroll=8)

        def second(t, carry):
            a = lax.rem(list_ref[2, t], local_tiles)
            ladder = jnp.dot(lv_ref[a], half[t], preferred_element_type=jnp.float32)
            inverse = inverse_at(t, list_ref, occ_ref, row_ref, column_ref)
            base_ref[t] = amp_ref[t].astype(jnp.float32) + ladder * inverse
            return carry

        lax.fori_loop(0, tiles, second, 0, unroll=8)

        def turn(g, carry):
            turned_ref[g] = cv_ref[g].astype(jnp.float32).T.astype(jnp.bfloat16)
            return carry

        lax.fori_loop(0, domains, turn, 0, unroll=2)

    return pl.pallas_call(
        kernel,
        out_shape=(sds(amplitudes.shape, jnp.float32), sds(cycle_virtual.shape, jnp.bfloat16)),
        in_specs=[spec(SMEM)] * 2 + [spec()] * 6,
        out_specs=(spec(), spec()),
        scratch_shapes=[VMEM(amplitudes.shape, jnp.bfloat16)],
        compiler_params=params(),
        name="ladder",
    )(tile_list, energies[0], amplitudes, ladder_virtual, ladder_domain, energies[1], energies[2], cycle_virtual)


def finish(tile_list, position, returned, cycle_turned, cycle_occupied, base, energies):
    tiles, width, domain = base.shape
    bounds = [tiles * j // CHUNKS for j in range(CHUNKS + 1)]
    pieces = list(zip(bounds[:-1], bounds[1:]))

    def kernel(
        list_ref,
        pos_ref,
        occ_ref,
        row_ref,
        column_ref,
        ret_ref,
        cv_ref,
        co_ref,
        base_ref,
        out_ref,
        base,
        out,
        sem,
        out_sem,
    ):
        loads, stores = [], []
        for j, (low, high) in enumerate(pieces):
            piece = pl.ds(low, high - low)
            loads.append(pltpu.make_async_copy(base_ref.at[piece], base.at[piece], sem.at[j, 0]))
            stores.append(pltpu.make_async_copy(out.at[piece], out_ref.at[piece], out_sem.at[j]))

        for load in loads:
            load.start()

        def one(t, carry):
            slot = pos_ref[t]
            row = pl.multiple_of(lax.rem(slot, CAP) * width, width)
            scaled = ret_ref[lax.div(slot, CAP), pl.ds(row, width), :].astype(jnp.float32) * co_ref[pl.ds(list_ref[1, t], 1), :]
            term = jnp.dot(scaled.astype(jnp.bfloat16), cv_ref[list_ref[3, t]], preferred_element_type=jnp.float32)
            inverse = inverse_at(t, list_ref, occ_ref, row_ref, column_ref)
            out[t] = (base[t] + term * inverse).astype(jnp.bfloat16)
            return carry

        for j, (low, high) in enumerate(pieces):
            loads[j].wait()
            lax.fori_loop(low, high, one, 0, unroll=high - low)
            stores[j].start()
        for copy in stores:
            copy.wait()

    return pl.pallas_call(
        kernel,
        out_shape=sds(base.shape, jnp.bfloat16),
        in_specs=[spec(SMEM)] * 3 + [spec()] * 5 + [spec(pltpu.HBM)],
        out_specs=spec(pltpu.HBM),
        scratch_shapes=[
            VMEM((tiles, width, domain), jnp.float32),
            VMEM((tiles, width, domain), jnp.bfloat16),
            pltpu.SemaphoreType.DMA((len(pieces), 2)),
            pltpu.SemaphoreType.DMA((len(pieces),)),
        ],
        compiler_params=params(),
        name="finish",
    )(tile_list, position, *energies, near(returned), cycle_turned, cycle_occupied, far(base))


def body(
    amplitudes,
    tile_list,
    ladder_virtual_integrals,
    ladder_domain_integrals,
    cycle_virtual,
    cycle_occupied,
    cycle_core,
    occ_energy,
    vir_energy,
):
    tiles, width, domain = amplitudes.shape
    owners = lax.axis_size("occ")
    local_tiles = ladder_virtual_integrals.shape[0]
    groups = -(-occ_energy.shape[0] // owners) * local_tiles
    vir_index = lax.axis_index("vir")
    local_energy = lax.dynamic_slice_in_dim(vir_energy, vir_index * local_tiles * width, local_tiles * width)
    row_energy = jnp.broadcast_to(local_energy.reshape(local_tiles, width, 1), (local_tiles, width, domain))
    column_energy = vir_energy.reshape(-1, domain)

    tile_list = tile_list.T
    cycle_occupied = cycle_occupied.astype(jnp.float32)
    send, position = pack(amplitudes, tile_list, owners, local_tiles)
    received = lax.all_to_all(send, "occ", split_axis=0, concat_axis=0, tiled=True)
    virtual_all = lax.all_gather(cycle_virtual, "vir", axis=0, tiled=True)
    energies = (occ_energy, row_energy, column_energy)
    answers = owner_core(received, virtual_all, cycle_occupied, cycle_core, width, groups)
    returned = lax.all_to_all(answers, "occ", split_axis=0, concat_axis=0, tiled=True)
    domain_own, _ = lax.optimization_barrier((ladder_domain_integrals, virtual_all))
    domain_all = lax.all_gather(domain_own, "vir", axis=0, tiled=True)
    base, turned = ladder_part(
        tile_list, amplitudes, ladder_virtual_integrals, domain_all, energies, virtual_all
    )
    return finish(tile_list, position, returned, turned, cycle_occupied, base, energies)


def solution(mesh):
    tile_spec = P(("occ", "vir"), None, None)
    return jax.shard_map(
        body,
        mesh=mesh,
        in_specs=(tile_spec, P(("occ", "vir"), None), P("vir"), P("vir"), P("vir"), P(), P(), P(), P()),
        out_specs=tile_spec,
        check_vma=False,
    )
```

```python
import jax
import jax.numpy as jnp
from jax import lax
from jax.experimental import pallas as pl
from jax.experimental.pallas import tpu as pltpu
from jax.sharding import PartitionSpec as P

CAP = 2
META = 2
FIELDS = 4 * CAP
VMEM_LIMIT = 20 * 2**20
CHUNKS = 4
SMEM = pltpu.SMEM
VMEM = pltpu.VMEM


def sds(shape, dtype):
    return jax.ShapeDtypeStruct(shape, dtype)


def spec(space=VMEM):
    return pl.BlockSpec(memory_space=space)


def near(x):
    return pltpu.with_memory_space_constraint(x, pltpu.VMEM)


def far(x):
    return pltpu.with_memory_space_constraint(x, pltpu.HBM)


def params():
    return pltpu.CompilerParams(vmem_limit_bytes=VMEM_LIMIT)


def pack(amplitudes, tile_list, owners, local_tiles):
    tiles, width, domain = amplitudes.shape
    rows = CAP * width

    def kernel(list_hbm, amp_ref, out_ref, pos_ref, count, list_ref, ids_ref, amp, meta, list_sem, load_sem, tile_sem, meta_sem):
        list_copy = pltpu.make_async_copy(list_hbm, list_ref, list_sem.at[0])
        list_copy.start()
        ids_copy = pltpu.make_async_copy(list_hbm, ids_ref, list_sem.at[1])
        ids_copy.start()
        part = tiles // CHUNKS
        loads = []
        for j in range(CHUNKS):
            piece = pl.ds(j * part, part)
            loads.append(pltpu.make_async_copy(amp_ref.at[piece], amp.at[piece], load_sem.at[j]))
            loads[j].start()

        message = out_ref.reshape(owners, rows + META, domain)

        def clear(o, carry):
            count[o] = 0
            return carry

        lax.fori_loop(0, owners, clear, 0, unroll=8)

        def place(t, carry):
            owner = lax.rem(list_ref[0, t], owners)
            rank = count[owner]
            count[owner] = rank + 1
            pos_ref[t] = owner * CAP + rank
            slot = message.at[owner, pl.ds(pl.multiple_of(rank * width, width), width)]
            pltpu.make_async_copy(amp.at[t], slot, tile_sem).start()
            return carry

        list_copy.wait()
        for j, load in enumerate(loads):
            load.wait()
            lax.fori_loop(j * part, (j + 1) * part, place, 0, unroll=16)
        ids_copy.wait()
        ids = ids_ref[...]
        i, k = ids[0:1], ids[1:2]
        owner = jnp.broadcast_to(lax.rem(i, owners).astype(jnp.float32), (tiles, tiles))
        earlier = lax.broadcasted_iota(jnp.int32, (tiles, tiles), 0) < lax.broadcasted_iota(
            jnp.int32, (tiles, tiles), 1
        )
        same = jnp.where((owner == owner.T) & earlier, 1.0, 0.0)
        rank = jnp.sum(same, axis=0, keepdims=True)
        key = lax.div(i, owners) * local_tiles + lax.rem(ids[2:3], local_tiles) + 1
        fields = [v.astype(jnp.float32) for v in (key, lax.div(k, 16), lax.rem(k, 16), ids[3:4])]
        lane = lax.broadcasted_iota(jnp.int32, (domain, tiles), 0)
        row_owner = lax.broadcasted_iota(jnp.int32, (owners * META, tiles), 0) // META
        total = jnp.zeros((owners * META, domain), jnp.float32)
        for c in range(CAP):
            mine = (row_owner.astype(jnp.float32) == owner[0:1]) & (rank == float(c))
            table = jnp.zeros((domain, tiles), jnp.float32)
            for f, value in enumerate(fields):
                table = jnp.where(lane == 4 * c + f, value, table)
            total += lax.dot_general(
                jnp.where(mine, 1.0, 0.0).astype(jnp.bfloat16),
                table.astype(jnp.bfloat16),
                (((1,), (1,)), ((), ())),
                preferred_element_type=jnp.float32,
            )
        meta.reshape(owners * META, domain)[...] = total.astype(jnp.bfloat16)
        meta_copy = pltpu.make_async_copy(meta, out_ref.at[:, pl.ds(rows // META, 1)], meta_sem)
        meta_copy.start()
        meta_copy.wait()
        pltpu.make_async_copy(amp, amp_ref, tile_sem).wait()

    return pl.pallas_call(
        kernel,
        out_shape=(pltpu.HBM((owners, rows // META + 1, META, domain), jnp.bfloat16), sds((tiles,), jnp.int32)),
        in_specs=[spec(pltpu.HBM), spec(pltpu.HBM)],
        out_specs=(spec(pltpu.HBM), spec(SMEM)),
        scratch_shapes=[
            SMEM((owners,), jnp.int32),
            SMEM(tile_list.shape, jnp.int32),
            VMEM(tile_list.shape, jnp.int32),
            VMEM((tiles, width, domain), jnp.bfloat16),
            VMEM((owners, 1, META, domain), jnp.bfloat16),
            pltpu.SemaphoreType.DMA((2,)),
            pltpu.SemaphoreType.DMA((CHUNKS,)),
            pltpu.SemaphoreType.DMA,
            pltpu.SemaphoreType.DMA,
        ],
        compiler_params=params(),
        name="pack",
    )(far(tile_list), far(amplitudes))


def owner_core(received, cycle_virtual, cycle_occupied, cycle_core, width, groups):
    sources, _, _, domain = received.shape
    rank = cycle_core.shape[0]
    rows = CAP * width

    def kernel(got_ref, cv_ref, co_ref, core_ref, out_ref, meta, ids_v, ids, sums, cores, sem, out_sem):
        got = got_ref.reshape(sources, rows + META, domain)
        meta[...] = got_ref[:, rows // META, 0, :].astype(jnp.float32)
        ids_v[...] = meta[...].T[0:FIELDS].astype(jnp.int32)
        ids_copy = pltpu.make_async_copy(ids_v, ids, sem)
        ids_copy.start()
        sums[...] = jnp.zeros_like(sums)
        ids_copy.wait()

        def add(s, carry):
            for c in range(CAP):
                key = ids[4 * c, s]
                k = ids[4 * c + 1, s] * 16 + ids[4 * c + 2, s]
                g = ids[4 * c + 3, s]
                tile = got[s, c * width : (c + 1) * width, :]
                one = jnp.dot(tile, cv_ref[g], preferred_element_type=jnp.float32)
                sums[key] += one * co_ref[pl.ds(k, 1), :]
            return carry

        lax.fori_loop(0, sources, add, 0, unroll=64)
        grouped = sums[...].astype(jnp.bfloat16).reshape((groups + 1) * width, rank)
        core = jnp.dot(grouped, core_ref[...], preferred_element_type=jnp.float32)
        cores[...] = core.astype(jnp.bfloat16).reshape(cores.shape)

        def answer(s, carry):
            for c in range(CAP):
                slot = out_ref.at[s, pl.ds(c * width, width)]
                pltpu.make_async_copy(cores.at[ids[4 * c, s]], slot, out_sem).start()
            return carry

        lax.fori_loop(0, sources, answer, 0, unroll=4)
        pltpu.make_async_copy(out_ref, out_ref, out_sem).wait()

    return pl.pallas_call(
        kernel,
        out_shape=pltpu.HBM((sources, rows, rank), jnp.bfloat16),
        in_specs=[spec()] * 4,
        out_specs=spec(pltpu.HBM),
        scratch_shapes=[
            VMEM((sources, domain), jnp.float32),
            VMEM((FIELDS, sources), jnp.int32),
            SMEM((FIELDS, sources), jnp.int32),
            VMEM((groups + 1, width, rank), jnp.float32),
            VMEM((groups + 1, width, rank), jnp.bfloat16),
            pltpu.SemaphoreType.DMA,
            pltpu.SemaphoreType.DMA,
        ],
        compiler_params=params(),
        name="owner_core",
    )(near(received), near(cycle_virtual), near(cycle_occupied), near(cycle_core))


def inverse_at(t, list_ref, occ_ref, row_ref, column_ref):
    a = lax.rem(list_ref[2, t], row_ref.shape[0])
    occ = occ_ref[list_ref[0, t]] + occ_ref[list_ref[1, t]]
    return 1.0 / (row_ref[a] + column_ref[pl.ds(list_ref[3, t], 1), :] - occ)


def ladder_part(tile_list, amplitudes, ladder_virtual, ladder_domain, energies, cycle_virtual):
    tiles, width, domain = amplitudes.shape
    local_tiles = ladder_virtual.shape[0]
    domains = cycle_virtual.shape[0]

    def kernel(list_ref, occ_ref, amp_ref, lv_ref, ld_ref, row_ref, column_ref, cv_ref, base_ref, turned_ref, half):
        def first(t, carry):
            part = jnp.dot(amp_ref[t], ld_ref[list_ref[3, t]], preferred_element_type=jnp.float32)
            half[t] = part.astype(jnp.bfloat16)
            return carry

        lax.fori_loop(0, tiles, first, 0, unroll=8)

        def second(t, carry):
            a = lax.rem(list_ref[2, t], local_tiles)
            ladder = jnp.dot(lv_ref[a], half[t], preferred_element_type=jnp.float32)
            inverse = inverse_at(t, list_ref, occ_ref, row_ref, column_ref)
            base_ref[t] = amp_ref[t].astype(jnp.float32) + ladder * inverse
            return carry

        lax.fori_loop(0, tiles, second, 0, unroll=8)

        def turn(g, carry):
            turned_ref[g] = cv_ref[g].astype(jnp.float32).T.astype(jnp.bfloat16)
            return carry

        lax.fori_loop(0, domains, turn, 0, unroll=2)

    return pl.pallas_call(
        kernel,
        out_shape=(sds(amplitudes.shape, jnp.float32), sds(cycle_virtual.shape, jnp.bfloat16)),
        in_specs=[spec(SMEM)] * 2 + [spec()] * 6,
        out_specs=(spec(), spec()),
        scratch_shapes=[VMEM(amplitudes.shape, jnp.bfloat16)],
        compiler_params=params(),
        name="ladder",
    )(tile_list, energies[0], amplitudes, ladder_virtual, ladder_domain, energies[1], energies[2], cycle_virtual)


def finish(tile_list, position, returned, cycle_turned, cycle_occupied, base, energies):
    tiles, width, domain = base.shape
    bounds = [0, tiles // 2, tiles]
    pieces = list(zip(bounds[:-1], bounds[1:]))

    def kernel(
        list_ref,
        pos_ref,
        occ_ref,
        row_ref,
        column_ref,
        ret_ref,
        cv_ref,
        co_ref,
        base_ref,
        out_ref,
        base,
        out,
        sem,
        out_sem,
    ):
        loads, stores = [], []
        for j, (low, high) in enumerate(pieces):
            piece = pl.ds(low, high - low)
            loads.append(pltpu.make_async_copy(base_ref.at[piece], base.at[piece], sem.at[j, 0]))
            stores.append(pltpu.make_async_copy(out.at[piece], out_ref.at[piece], out_sem.at[j]))

        for load in loads:
            load.start()

        def one(t, carry):
            slot = pos_ref[t]
            row = pl.multiple_of(lax.rem(slot, CAP) * width, width)
            scaled = ret_ref[lax.div(slot, CAP), pl.ds(row, width), :].astype(jnp.float32) * co_ref[pl.ds(list_ref[1, t], 1), :]
            term = jnp.dot(scaled.astype(jnp.bfloat16), cv_ref[list_ref[3, t]], preferred_element_type=jnp.float32)
            inverse = inverse_at(t, list_ref, occ_ref, row_ref, column_ref)
            out[t] = (base[t] + term * inverse).astype(jnp.bfloat16)
            return carry

        for j, (low, high) in enumerate(pieces):
            loads[j].wait()
            lax.fori_loop(low, high, one, 0, unroll=high - low)
            stores[j].start()
        for copy in stores:
            copy.wait()

    return pl.pallas_call(
        kernel,
        out_shape=sds(base.shape, jnp.bfloat16),
        in_specs=[spec(SMEM)] * 3 + [spec()] * 5 + [spec(pltpu.HBM)],
        out_specs=spec(pltpu.HBM),
        scratch_shapes=[
            VMEM((tiles, width, domain), jnp.float32),
            VMEM((tiles, width, domain), jnp.bfloat16),
            pltpu.SemaphoreType.DMA((len(pieces), 2)),
            pltpu.SemaphoreType.DMA((len(pieces),)),
        ],
        compiler_params=params(),
        name="finish",
    )(tile_list, position, *energies, near(returned), cycle_turned, cycle_occupied, far(base))


def body(
    amplitudes,
    tile_list,
    ladder_virtual_integrals,
    ladder_domain_integrals,
    cycle_virtual,
    cycle_occupied,
    cycle_core,
    occ_energy,
    vir_energy,
):
    tiles, width, domain = amplitudes.shape
    owners = lax.axis_size("occ")
    local_tiles = ladder_virtual_integrals.shape[0]
    groups = -(-occ_energy.shape[0] // owners) * local_tiles
    vir_index = lax.axis_index("vir")
    local_energy = lax.dynamic_slice_in_dim(vir_energy, vir_index * local_tiles * width, local_tiles * width)
    row_energy = jnp.broadcast_to(local_energy.reshape(local_tiles, width, 1), (local_tiles, width, domain))
    column_energy = vir_energy.reshape(-1, domain)

    tile_list = tile_list.T
    cycle_occupied = cycle_occupied.astype(jnp.float32)
    send, position = pack(amplitudes, tile_list, owners, local_tiles)
    received = lax.all_to_all(send, "occ", split_axis=0, concat_axis=0, tiled=True)
    virtual_all = lax.all_gather(cycle_virtual, "vir", axis=0, tiled=True)
    energies = (occ_energy, row_energy, column_energy)
    answers = owner_core(received, virtual_all, cycle_occupied, cycle_core, width, groups)
    returned = lax.all_to_all(answers, "occ", split_axis=0, concat_axis=0, tiled=True)
    domain_own, _ = lax.optimization_barrier((ladder_domain_integrals, virtual_all))
    domain_all = lax.all_gather(domain_own, "vir", axis=0, tiled=True)
    base, turned = ladder_part(
        tile_list, amplitudes, ladder_virtual_integrals, domain_all, energies, virtual_all
    )
    return finish(tile_list, position, returned, turned, cycle_occupied, base, energies)


def solution(mesh):
    tile_spec = P(("occ", "vir"), None, None)
    return jax.shard_map(
        body,
        mesh=mesh,
        in_specs=(tile_spec, P(("occ", "vir"), None), P("vir"), P("vir"), P("vir"), P(), P(), P(), P()),
        out_specs=tile_spec,
        check_vma=False,
    )
```
